768 devices in a mesh: seq: 64 (over y, x, core), head: 12 (over z).
Axes of the slice: x: 4, y: 8, z: 12, core: 2. Of those that a mesh axis runs over, the one named last changes fastest.
Arguments:
- query_act: bfloat16 [16384, 4608], P('seq', 'head'), may hold values from -0.59765625 to 0.59765625
- key_act: bfloat16 [16384, 4608], P('seq', 'head'), may hold values from -0.59765625 to 0.59765625
- value_act: bfloat16 [16384, 4608], P('seq', 'head'), may hold values from -0.59765625 to 0.59765625
- grad_output: bfloat16 [16384, 4608], P('seq', 'head'), may hold values from -0.375 to 0.375
- log_decay: float32 [16384, 36], P('seq', 'head'), may hold values from -1 to 0
- w_query: bfloat16 [6144, 4608], P(None, 'head'), may hold values from -0.0625 to 0.0625
- w_key: bfloat16 [6144, 4608], P(None, 'head'), may hold values from -0.0625 to 0.0625
Outputs:
- grad_input: bfloat16 [6144, 16384], P('head', 'seq')
The draws below stay inside these ranges and needn't reach their ends.
All inputs are finite; a program needn't handle non-finite values.
Results may differ from the reference program's by a relative error of at most 0.015.
Values may be sent and summed in bfloat16 or wider, within the bound.
A program may use at most 128 MiB of HBM per device.

```python
import math
import jax
import jax.numpy as jnp
from jax import lax

D = 6144
HD = 128
HEADS_DEV = 3
TOK_DEV = 256
ATTENTION_HEADS = 36
SEQUENCE_TOKENS = 16384
N_SEQ = 64
N_HEAD = 12


def draw_log_decay(key, part):
    random_split_keys = jax.random.split(jax.random.fold_in(key, 7), 5)
    fast_share = 0.5
    fast_heads = jax.random.bernoulli(random_split_keys[0], fast_share, (ATTENTION_HEADS,))
    fast_rate = jnp.exp(jax.random.uniform(random_split_keys[1], (ATTENTION_HEADS,), jnp.float32, math.log(1.0 / 50.0), math.log(1.0 / 30.0)))
    slow_rate = jnp.full((ATTENTION_HEADS,), 0.5 / SEQUENCE_TOKENS, jnp.float32)
    baseline_decay_rate = jnp.where(fast_heads, fast_rate, slow_rate)
    random_noise = jnp.exp(jax.random.uniform(random_split_keys[2], (SEQUENCE_TOKENS, ATTENTION_HEADS), jnp.float32, -math.log(2.0), math.log(2.0)))
    spike_row_count = jax.random.randint(random_split_keys[3], (3,), 0, SEQUENCE_TOKENS)
    spike_lengths = -jnp.log(1.0 - jax.random.uniform(random_split_keys[4], (3, ATTENTION_HEADS), jnp.float32, 0.2, 0.4))
    decay_spikes = jnp.zeros((SEQUENCE_TOKENS, ATTENTION_HEADS), jnp.float32).at[spike_row_count].add(spike_lengths)
    return (-(baseline_decay_rate[None, :] * random_noise) - decay_spikes).astype(jnp.float32)


def block_levels(rng, shape, cuts, smallest, largest):
    loudness = 1.0
    for dim, blocks in cuts:
        steps = jax.random.uniform(jax.random.fold_in(jax.random.fold_in(rng, 6), dim), (blocks,), jnp.float32, smallest / len(cuts), largest / len(cuts))
        loudness = loudness * jnp.repeat(jnp.exp(steps), shape[dim] // blocks).reshape((-1,) + (1,) * (len(shape) - 1 - dim))
    return loudness


def noise(key, shape, width, most, cuts=(), kind=jnp.bfloat16):
    array = width * jax.random.normal(key, shape, jnp.float32)
    if cuts:
        array = array * block_levels(key, shape, cuts, -0.22, 0.18)
    return jnp.clip(array, -most, most).astype(kind)


def setup_inputs(seed: int = 0) -> dict:
    arg_keys = jax.random.split(jax.random.key(seed), 8)
    query_act = noise(arg_keys[0], (SEQUENCE_TOKENS, ATTENTION_HEADS * HD), 0.1, 0.59765625, ((0, 64), (1, 12)))
    key_act = noise(arg_keys[1], (SEQUENCE_TOKENS, ATTENTION_HEADS * HD), 0.1, 0.59765625, ((0, 64), (1, 12)))
    value_act = noise(arg_keys[2], (SEQUENCE_TOKENS, ATTENTION_HEADS * HD), 0.1, 0.59765625, ((0, 64), (1, 12)))
    grad_output = noise(arg_keys[3], (SEQUENCE_TOKENS, ATTENTION_HEADS * HD), (8.0 / SEQUENCE_TOKENS ** 0.5), 0.375, ((0, 64), (1, 12)))
    log_decay = draw_log_decay(jax.random.fold_in(arg_keys[7], 71), 0)
    w_query = noise(arg_keys[5], (D, ATTENTION_HEADS * HD), (2 * ATTENTION_HEADS * HD) ** -0.5, 0.0625, ((1, 12),))
    w_key = noise(arg_keys[6], (D, ATTENTION_HEADS * HD), (2 * ATTENTION_HEADS * HD) ** -0.5, 0.0625, ((1, 12),))
    return dict(query_act=query_act, key_act=key_act, value_act=value_act, grad_output=grad_output, log_decay=log_decay, w_query=w_query, w_key=w_key)


def to_bf16(values):
    return lax.optimization_barrier(values.astype(jnp.bfloat16))


def block_grads(queries, keys_blk, values_blk, grads_blk, cumlog, state_in, grad_in):
    f32 = jnp.float32
    span = cumlog.shape[0]
    last_log = cumlog[-1]
    log_gap = cumlog[:, None, :] - cumlog[None, :, :]
    positions = jnp.arange(span)
    causal_mask = positions[:, None] >= positions[None, :]
    decay_mat = jnp.where(causal_mask[:, :, None], jnp.exp(jnp.minimum(log_gap, 0.0)), 0.0)
    dot_scores = jnp.einsum("the,she->tsh", grads_blk.astype(f32), values_blk.astype(f32))
    weighted = to_bf16(dot_scores * decay_mat).astype(f32)
    dq_local = jnp.einsum("tsh,shd->thd", weighted, keys_blk.astype(f32))
    dk_local = jnp.einsum("tsh,thd->shd", weighted, queries.astype(f32))
    state_bf = to_bf16(state_in).astype(f32)
    grad_bf = to_bf16(grad_in).astype(f32)
    dq_carry = jnp.einsum("the,hde->thd", grads_blk.astype(f32), state_bf) * jnp.exp(cumlog)[:, :, None]
    dk_carry = jnp.einsum("the,hde->thd", values_blk.astype(f32), grad_bf) * jnp.exp(last_log[None, :] - cumlog)[:, :, None]
    return to_bf16(dq_local + dq_carry), to_bf16(dk_local + dk_carry)


def reference(query_act, key_act, value_act, grad_output, log_decay, w_query, w_key):
    f32 = jnp.float32
    shape_four = (N_SEQ, TOK_DEV, ATTENTION_HEADS, HD)
    queries = query_act.reshape(shape_four)
    keys_all = key_act.reshape(shape_four)
    values_all = value_act.reshape(shape_four)
    grads_all = grad_output.reshape(shape_four)
    cumlog = jnp.cumsum(log_decay.reshape(N_SEQ, TOK_DEV, ATTENTION_HEADS).astype(f32), axis=1)
    last_log = cumlog[:, -1]
    decay_total = jnp.exp(last_log)
    key_weighted = to_bf16(keys_all.astype(f32) * jnp.exp(last_log[:, None, :] - cumlog)[..., None]).astype(f32)
    query_weighted = to_bf16(queries.astype(f32) * jnp.exp(cumlog)[..., None]).astype(f32)
    local_states = jnp.einsum("nthd,nthe->nhde", key_weighted, values_all.astype(f32))
    local_grads = jnp.einsum("nthd,nthe->nhde", query_weighted, grads_all.astype(f32))

    def forward_step(running, inputs):
        total, state = inputs
        return total[:, None, None] * running + state, running

    start_state = jnp.zeros((ATTENTION_HEADS, HD, HD), f32)
    _, states_in = lax.scan(forward_step, start_state, (decay_total, local_states))
    _, grads_in = lax.scan(forward_step, start_state, (decay_total, local_grads), reverse=True)
    grad_query, grad_key = lax.map(lambda packed: block_grads(*packed),
                                   (queries, keys_all, values_all, grads_all, cumlog, states_in, grads_in))
    dq_flat = grad_query.reshape(SEQUENCE_TOKENS, ATTENTION_HEADS * HD)
    dk_flat = grad_key.reshape(SEQUENCE_TOKENS, ATTENTION_HEADS * HD)
    group_width = HEADS_DEV * HD
    dims = (((1,), (1,)), ((), ()))
    summed = jnp.zeros((D, SEQUENCE_TOKENS), f32)
    for group_index in range(N_HEAD):
        lower = group_index * group_width
        upper = lower + group_width
        partial_term = lax.dot_general(w_query[:, lower:upper], dq_flat[:, lower:upper], dims, preferred_element_type=f32)
        partial_term = partial_term + lax.dot_general(w_key[:, lower:upper], dk_flat[:, lower:upper], dims, preferred_element_type=f32)
        summed = summed + to_bf16(partial_term).astype(f32)
    return summed.astype(jnp.bfloat16)
```

```python
import functools

import jax
import jax.numpy as jnp
from jax import lax
from jax.experimental import pallas as pl
from jax.experimental.pallas import tpu as pltpu
from jax.sharding import Mesh
from jax.sharding import PartitionSpec as P

SEQ = ("seq_0", "seq_1", "seq_2")
F32 = jnp.float32
BF16 = jnp.bfloat16
MESH = pl.DeviceIdType.MESH
LANES = 128
PIECES = 4


def nn(a, b):
    return lax.dot_general(a, b, (((1,), (0,)), ((), ())), preferred_element_type=F32)


def nt(a, b):
    return lax.dot_general(a, b, (((1,), (1,)), ((), ())), preferred_element_type=F32)


def kernel(
    dims,
    q_hbm, k_hbm, v_hbm, g_hbm, ld_hbm, wq_hbm, wk_hbm,
    out_ref,
    q_v, k_v, v_v, g_v, ld_v, wq_v, wk_v,
    buf_a, rec_a, lbuf_a, lrec_a,
    exc, wgt, tot_b, rec_b, lbuf_b, lrec_b,
    buf_c, rec_c,
    loc, xt, sbuf, rbuf,
    in_sem,
    sa_sem, ra_sem, sla_sem, rla_sem,
    sb_sem, rb_sem, slb_sem, rlb_sem,
    sc_sem, rc_sem,
    sz_sem, rz_sem,
):
    ny, nr, nc, nz, nh, span, chunk = dims
    width = LANES
    hw = nh * width
    part = width // nr
    half = nz // 2
    rows = chunk // PIECES
    y = lax.axis_index("seq_0")
    r = lax.axis_index("seq_1") * nc + lax.axis_index("seq_2")
    z = lax.axis_index("head")

    def row_peer(p):
        return {"seq_1": p // nc, "seq_2": p % nc}

    loads = []
    for i, (src, dst) in enumerate(
        ((ld_hbm, ld_v), (k_hbm, k_v), (v_hbm, v_v), (q_hbm, q_v), (g_hbm, g_v), (wq_hbm, wq_v), (wk_hbm, wk_v))
    ):
        load = pltpu.make_async_copy(src, dst, in_sem.at[i])
        load.start()
        loads.append(load)

    barrier = pltpu.get_barrier_semaphore()
    for i in range(1, nr):
        pl.semaphore_signal(barrier, inc=1, device_id=row_peer((r + i) % nr), device_id_type=MESH)
    for i in range(1, ny):
        pl.semaphore_signal(barrier, inc=1, device_id={"seq_0": (y + i) % ny}, device_id_type=MESH)
    for step in (1, nz - 1):
        pl.semaphore_signal(barrier, inc=1, device_id={"head": (z + step) % nz}, device_id_type=MESH)

    loads[0].wait()
    ld = jnp.concatenate([ld_v[...], jnp.zeros((8 - nh, span), F32)], axis=0)
    first = lax.broadcasted_iota(jnp.int32, (span, span), 0)
    second = lax.broadcasted_iota(jnp.int32, (span, span), 1)
    causal = first <= second
    cum = lax.dot_general(
        ld, causal.astype(F32), (((1,), (0,)), ((), ())), precision=lax.Precision.HIGHEST, preferred_element_type=F32
    )
    last = cum[:, span - 1 : span]
    lbuf_a[...] = jnp.broadcast_to(last, (8, LANES))
    up_decay = jnp.exp(cum)
    down_decay = jnp.exp(jnp.minimum(last - cum, 0.0))

    pl.semaphore_wait(barrier, nr + ny)

    def row_copy(src, dst, ssem, rsem, i, use_own):
        to = (r + i) % nr
        return pltpu.make_async_remote_copy(
            src_ref=src.at[to] if use_own else src,
            dst_ref=dst.at[r],
            send_sem=ssem.at[i - 1],
            recv_sem=rsem.at[r],
            device_id=row_peer(to),
            device_id_type=MESH,
        )

    def row_arrival(dst, rsem, i):
        frm = (r + i) % nr
        return pltpu.make_async_remote_copy(
            src_ref=dst.at[frm],
            dst_ref=dst.at[frm],
            send_sem=rsem.at[frm],
            recv_sem=rsem.at[frm],
            device_id=row_peer(frm),
            device_id_type=MESH,
        )

    sends = []

    def go(copy):
        copy.start()
        sends.append(copy)

    for i in range(1, nr):
        go(row_copy(lbuf_a, lrec_a, sla_sem, rla_sem, i, False))
    lrec_a[r] = lbuf_a[...]

    def flipped(ref):
        return ref[...].astype(F32).T

    loads[1].wait()
    k_t = flipped(k_v)
    loads[2].wait()
    for h in range(nh):
        cols = slice(h * width, (h + 1) * width)
        kw = (k_t[cols, :] * down_decay[h : h + 1, :]).astype(BF16)
        state = nn(kw, v_v[:, cols]).astype(BF16)
        buf_a[:, 0, h] = state.reshape(nr, part, width)
    loads[3].wait()
    q_t = flipped(q_v)
    loads[4].wait()
    for h in range(nh):
        cols = slice(h * width, (h + 1) * width)
        qw = (q_t[cols, :] * up_decay[h : h + 1, :]).astype(BF16)
        state = nn(qw, g_v[:, cols]).astype(BF16)
        buf_a[:, 1, h] = state.reshape(nr, part, width)
    for i in range(1, nr):
        go(row_copy(buf_a, rec_a, sa_sem, ra_sem, i, True))
    rec_a[r] = buf_a[r]

    for i in range(1, nr):
        row_arrival(lrec_a, rla_sem, i).wait_recv()
    ahead = jnp.zeros((8, LANES), F32)
    for p in range(nr):
        wgt[0, p] = jnp.exp(ahead)
        ahead = ahead + lrec_a[p]
    lbuf_b[...] = ahead
    behind = jnp.zeros((8, LANES), F32)
    for p in reversed(range(nr)):
        wgt[1, p] = jnp.exp(behind)
        behind = behind + lrec_a[p]

    def column_copy(src, dst, ssem, rsem, i, sided):
        return pltpu.make_async_remote_copy(
            src_ref=src.at[(y + i) // ny] if sided else src,
            dst_ref=dst.at[y],
            send_sem=ssem.at[i - 1],
            recv_sem=rsem.at[y],
            device_id={"seq_0": (y + i) % ny},
            device_id_type=MESH,
        )

    def column_arrival(dst, rsem, i):
        frm = (y + i) % ny
        return pltpu.make_async_remote_copy(
            src_ref=dst.at[frm],
            dst_ref=dst.at[frm],
            send_sem=rsem.at[frm],
            recv_sem=rsem.at[frm],
            device_id={"seq_0": frm},
            device_id_type=MESH,
        )

    for i in range(1, ny):
        go(column_copy(lbuf_b, lrec_b, slb_sem, rlb_sem, i, False))

    cum_t = cum.T
    k_b = k_t.astype(BF16)
    q_b = q_t.astype(BF16)

    def local_part(h):
        cols = slice(h * width, (h + 1) * width)
        gap = cum[h : h + 1, :] - cum_t[:, h : h + 1]
        decay = jnp.where(causal, jnp.exp(jnp.minimum(gap, 0.0)), 0.0)
        weighted = (nt(v_v[:, cols], g_v[:, cols]) * decay).astype(BF16)
        loc[0, h] = nn(k_b[cols, :], weighted)
        loc[1, h] = nt(q_b[cols, :], weighted)

    local_part(0)

    for i in range(1, nr):
        row_arrival(rec_a, ra_sem, i).wait_recv()
    for h in range(nh):
        run = jnp.zeros((part, width), F32)
        for p in range(nr):
            exc[0, p, h] = run
            run = jnp.exp(lrec_a[p, h : h + 1, :]) * run + rec_a[p, 0, h].astype(F32)
        tot_b[0, h] = run.astype(BF16)
        run = jnp.zeros((part, width), F32)
        for p in reversed(range(nr)):
            exc[1, p, h] = run
            run = jnp.exp(lrec_a[p, h : h + 1, :]) * run + rec_a[p, 1, h].astype(F32)
        tot_b[1, h] = run.astype(BF16)
    for i in range(1, ny):
        go(column_copy(tot_b, rec_b, sb_sem, rb_sem, i, True))

    for h in range(1, nh):
        local_part(h)

    for i in range(1, ny):
        column_arrival(lrec_b, rlb_sem, i).wait_recv()
    for i in range(1, ny):
        column_arrival(rec_b, rb_sem, i).wait_recv()

    def onward(p, run):
        decay = jnp.exp(lrec_b[p])
        return tuple(decay[h : h + 1, :] * run[h] + rec_b[p, h].astype(F32) for h in range(nh))

    empty = tuple(jnp.zeros((part, width), F32) for _ in range(nh))
    before = lax.fori_loop(0, y, onward, empty)
    after = lax.fori_loop(0, ny - 1 - y, lambda i, run: onward(ny - 1 - i, run), empty)
    for p in range(nr):
        for h in range(nh):
            buf_c[p, 0, h] = (wgt[0, p, h : h + 1, :] * before[h] + exc[0, p, h]).astype(BF16)
            buf_c[p, 1, h] = (wgt[1, p, h : h + 1, :] * after[h] + exc[1, p, h]).astype(BF16)
    for i in range(1, nr):
        go(row_copy(buf_c, rec_c, sc_sem, rc_sem, i, True))
    rec_c[r] = buf_c[r]
    g_t = flipped(g_v).astype(BF16)
    v_t = flipped(v_v).astype(BF16)
    for i in range(1, nr):
        row_arrival(rec_c, rc_sem, i).wait_recv()
    for h in range(nh):
        cols = slice(h * width, (h + 1) * width)
        state = rec_c[:, 0, h].reshape(width, width)
        xt[cols, :] = (loc[0, h] + nn(state, g_t[cols, :]) * up_decay[h : h + 1, :]).astype(BF16)
        state = rec_c[:, 1, h].reshape(width, width)
        xt[hw + h * width : hw + (h + 1) * width, :] = (
            loc[1, h] + nn(state, v_t[cols, :]) * down_decay[h : h + 1, :]
        ).astype(BF16)

    loads[5].wait()
    loads[6].wait()

    def own(dest, pc):
        span_rows = pl.ds(pl.multiple_of(dest * chunk + pc * rows, rows), rows)
        return nn(wq_v[span_rows, :], xt[0:hw, :]) + nn(wk_v[span_rows, :], xt[hw : 2 * hw, :])

    def ring_copy(way, step, pc):
        at = pl.ds(pc * rows, rows)
        return pltpu.make_async_remote_copy(
            src_ref=sbuf.at[way, step, at],
            dst_ref=rbuf.at[way, step, at],
            send_sem=sz_sem.at[way, step, pc],
            recv_sem=rz_sem.at[way, step, pc],
            device_id={"head": (z + (1 if way == 0 else nz - 1)) % nz},
            device_id_type=MESH,
        )

    def relay(way, step, pc, fresh):
        away = half - step
        dest = (z + (away if way == 0 else nz - away)) % nz
        value = own(dest, pc)
        at = pl.ds(pc * rows, rows)
        if not fresh:
            ring_copy(way, step - 1, pc).wait_recv()
            value = value + rbuf[way, step - 1, at, :].astype(F32)
        sbuf[way, step, at, :] = value.astype(BF16)
        ring_copy(way, step, pc).start()

    mid = PIECES // 2
    for i in range(mid):
        relay(0, 0, i, True)
        relay(1, 0, mid + i, True)
    for i in range(mid):
        relay(0, 1, mid + i, True)
        relay(1, 1, i, True)
    for i in range(mid):
        relay(0, 1, i, False)
        relay(1, 1, mid + i, False)

    def ring_step(step, carry):
        for i in range(PIECES):
            relay(0, step, (mid + i) % PIECES, False)
            relay(1, step, i, False)
        return carry

    lax.fori_loop(2, half, ring_step, 0)
    for i in range(PIECES):
        pc_up, pc_down = (mid + i) % PIECES, i
        for pc in (i,):
            at = pl.ds(pc * rows, rows)
            value = own(z, pc)
            ring_copy(0, half - 1, pc).wait_recv()
            ring_copy(1, half - 1, pc).wait_recv()
            value = value + rbuf[0, half - 1, at, :].astype(F32) + rbuf[1, half - 1, at, :].astype(F32)
            out_ref[at, :] = value.astype(BF16)

    for copy in sends:
        copy.wait_send()
    for way in range(2):
        for i in range(mid):
            ring_copy(way, 0, i + mid * way).wait_send()

    def drain(step, carry):
        for way in range(2):
            for pc in range(PIECES):
                ring_copy(way, step, pc).wait_send()
        return carry

    lax.fori_loop(1, half, drain, 0)


def shards(sizes, query_act, key_act, value_act, grad_output, log_decay, w_query, w_key):
    ny, nx, nc, nz = sizes
    span = query_act.shape[0]
    nh = log_decay.shape[1]
    width = query_act.shape[1] // nh
    hw = nh * width
    nr = nx * nc
    part = width // nr
    half = nz // 2
    features = w_query.shape[0]
    chunk = features // nz
    dims = (ny, nr, nc, nz, nh, span, chunk)
    vmem = pltpu.VMEM
    dma = pltpu.SemaphoreType.DMA
    scratch = [
        vmem((span, hw), BF16), vmem((span, hw), BF16), vmem((span, hw), BF16), vmem((span, hw), BF16),
        vmem((nh, span), F32), vmem((features, hw), BF16), vmem((features, hw), BF16),
        vmem((nr, 2, nh, part, width), BF16), vmem((nr, 2, nh, part, width), BF16),
        vmem((8, LANES), F32), vmem((nr, 8, LANES), F32),
        vmem((2, nr, nh, part, width), F32), vmem((2, nr, 8, LANES), F32),
        vmem((2, nh, part, width), BF16), vmem((ny, nh, part, width), BF16),
        vmem((8, LANES), F32), vmem((ny, 8, LANES), F32),
        vmem((nr, 2, nh, part, width), BF16), vmem((nr, 2, nh, part, width), BF16),
        vmem((2, nh, width, span), F32), vmem((2 * hw, span), BF16),
        vmem((2, half, chunk, span), BF16), vmem((2, half, chunk, span), BF16),
        dma((7,)),
        dma((nr - 1,)), dma((nr,)), dma((nr - 1,)), dma((nr,)),
        dma((ny - 1,)), dma((ny,)), dma((ny - 1,)), dma((ny,)),
        dma((nr - 1,)), dma((nr,)),
        dma((2, half, PIECES)), dma((2, half, PIECES)),
    ]
    hbm = pl.BlockSpec(memory_space=pl.ANY)
    return pl.pallas_call(
        functools.partial(kernel, dims),
        out_shape=jax.ShapeDtypeStruct((chunk, span), BF16),
        in_specs=[hbm] * 7,
        out_specs=pl.BlockSpec(memory_space=pltpu.VMEM),
        scratch_shapes=scratch,
        compiler_params=pltpu.CompilerParams(
            collective_id=0, has_side_effects=True, vmem_limit_bytes=60 * 1024 * 1024
        ),
        name="attention_backward",
    )(query_act, key_act, value_act, grad_output, log_decay.T, w_query, w_key)


def build(torus):
    sizes = tuple(torus.shape[a] for a in SEQ + ("head",))
    return jax.shard_map(
        functools.partial(shards, sizes),
        mesh=torus,
        in_specs=(
            P(SEQ, "head"),
            P(SEQ, "head"),
            P(SEQ, "head"),
            P(SEQ, "head"),
            P(SEQ, "head"),
            P(None, "head"),
            P(None, "head"),
        ),
        out_specs=P("head", SEQ),
        check_vma=False,
    )


def solution(mesh):
    torus = Mesh(
        mesh.devices.reshape(8, 4, 2, mesh.shape["head"]), ("seq_0", "seq_1", "seq_2", "head")
    )
    return build(torus)
```

```python
import functools

import jax
import jax.numpy as jnp
from jax import lax
from jax.experimental import pallas as pl
from jax.experimental.pallas import tpu as pltpu
from jax.sharding import Mesh
from jax.sharding import PartitionSpec as P

SEQ = ("seq_0", "seq_1", "seq_2")
F32 = jnp.float32
BF16 = jnp.bfloat16
MESH = pl.DeviceIdType.MESH
LANES = 128
PIECES = 4


def nn(a, b):
    return lax.dot_general(a, b, (((1,), (0,)), ((), ())), preferred_element_type=F32)


def nt(a, b):
    return lax.dot_general(a, b, (((1,), (1,)), ((), ())), preferred_element_type=F32)


def kernel(
    dims,
    q_hbm, k_hbm, v_hbm, g_hbm, ld_hbm, wq_hbm, wk_hbm,
    out_ref,
    q_v, k_v, v_v, g_v, ld_v, wq_v, wk_v,
    buf_a, rec_a, lbuf_a, lrec_a,
    exc, wgt, wgt_b, tot_b, rec_b, lbuf_b, lrec_b,
    buf_c, rec_c,
    loc, xt, sbuf, rbuf,
    in_sem,
    sa_sem, ra_sem, sla_sem, rla_sem,
    sb_sem, rb_sem, slb_sem, rlb_sem,
    sc_sem, rc_sem,
    sz_sem, rz_sem,
):
    ny, nr, nc, nz, nh, span, chunk = dims
    width = LANES
    hw = nh * width
    part = width // nr
    half = nz // 2
    rows = chunk // PIECES
    y = lax.axis_index("seq_0")
    r = lax.axis_index("seq_1") * nc + lax.axis_index("seq_2")
    z = lax.axis_index("head")

    def row_peer(p):
        return {"seq_1": p // nc, "seq_2": p % nc}

    loads = []
    for i, (src, dst) in enumerate(
        ((ld_hbm, ld_v), (k_hbm, k_v), (v_hbm, v_v), (q_hbm, q_v), (g_hbm, g_v), (wq_hbm, wq_v), (wk_hbm, wk_v))
    ):
        load = pltpu.make_async_copy(src, dst, in_sem.at[i])
        load.start()
        loads.append(load)

    barrier = pltpu.get_barrier_semaphore()
    for i in range(1, nr):
        pl.semaphore_signal(barrier, inc=1, device_id=row_peer((r + i) % nr), device_id_type=MESH)
    for i in range(1, ny):
        pl.semaphore_signal(barrier, inc=1, device_id={"seq_0": (y + i) % ny}, device_id_type=MESH)
    for step in (1, nz - 1):
        pl.semaphore_signal(barrier, inc=1, device_id={"head": (z + step) % nz}, device_id_type=MESH)

    loads[0].wait()
    ld = jnp.concatenate([ld_v[...], jnp.zeros((8 - nh, span), F32)], axis=0)
    first = lax.broadcasted_iota(jnp.int32, (span, span), 0)
    second = lax.broadcasted_iota(jnp.int32, (span, span), 1)
    causal = first <= second
    cum = lax.dot_general(
        ld, causal.astype(F32), (((1,), (0,)), ((), ())), precision=lax.Precision.HIGHEST, preferred_element_type=F32
    )
    last = cum[:, span - 1 : span]
    lbuf_a[...] = jnp.broadcast_to(last, (8, LANES))
    up_decay = jnp.exp(cum)
    down_decay = jnp.exp(jnp.minimum(last - cum, 0.0))

    pl.semaphore_wait(barrier, nr + ny)

    def row_copy(src, dst, ssem, rsem, i):
        return pltpu.make_async_remote_copy(
            src_ref=src, dst_ref=dst, send_sem=ssem, recv_sem=rsem,
            device_id=row_peer((r + i) % nr), device_id_type=MESH,
        )

    def column_copy(src, dst, ssem, rsem, i):
        return pltpu.make_async_remote_copy(
            src_ref=src, dst_ref=dst, send_sem=ssem, recv_sem=rsem,
            device_id={"seq_0": (y + i) % ny}, device_id_type=MESH,
        )

    def column_arrival(dst, rsem, i):
        frm = (y + i) % ny
        return pltpu.make_async_remote_copy(
            src_ref=dst.at[frm],
            dst_ref=dst.at[frm],
            send_sem=rsem.at[frm],
            recv_sem=rsem.at[frm],
            device_id={"seq_0": frm},
            device_id_type=MESH,
        )

    def row_arrival(dst, rsem, i):
        frm = (r + i) % nr
        return pltpu.make_async_remote_copy(
            src_ref=dst.at[frm],
            dst_ref=dst.at[frm],
            send_sem=rsem.at[frm],
            recv_sem=rsem.at[frm],
            device_id=row_peer(frm),
            device_id_type=MESH,
        )

    sends = []

    def go(copy):
        copy.start()
        sends.append(copy)

    for i in range(1, nr):
        go(row_copy(lbuf_a, lrec_a.at[r], sla_sem.at[i - 1], rla_sem.at[r], i))
    lrec_a[r] = lbuf_a[...]

    def flipped(ref):
        return ref[...].astype(F32).T

    def head(h):
        return slice(h * width, (h + 1) * width)

    loads[1].wait()
    k_t = flipped(k_v)
    loads[2].wait()
    loads[3].wait()
    q_t = flipped(q_v)
    loads[4].wait()
    for h in range(nh):
        kw = (k_t[head(h), :] * down_decay[h : h + 1, :]).astype(BF16)
        qw = (q_t[head(h), :] * up_decay[h : h + 1, :]).astype(BF16)
        buf_a[h, :, 0] = nn(kw, v_v[:, head(h)]).astype(BF16).reshape(nr, part, width)
        buf_a[h, :, 1] = nn(qw, g_v[:, head(h)]).astype(BF16).reshape(nr, part, width)
        for i in range(1, nr):
            go(row_copy(buf_a.at[h, (r + i) % nr], rec_a.at[h, r], sa_sem.at[h, i - 1], ra_sem.at[h, r], i))
        rec_a[h, r] = buf_a[h, r]

    for i in range(1, nr):
        row_arrival(lrec_a, rla_sem, i).wait_recv()
    ahead = jnp.zeros((8, LANES), F32)
    for p in range(nr):
        wgt[0, p] = jnp.exp(ahead)
        wgt[2, p] = jnp.exp(lrec_a[p])
        ahead = ahead + lrec_a[p]
    lbuf_b[...] = ahead
    for i in range(1, ny):
        go(column_copy(lbuf_b, lrec_b.at[y], slb_sem.at[i - 1], rlb_sem.at[y], i))
    behind = jnp.zeros((8, LANES), F32)
    for p in reversed(range(nr)):
        wgt[1, p] = jnp.exp(behind)
        behind = behind + lrec_a[p]

    cum_t = cum.T
    k_b = k_t.astype(BF16)
    q_b = q_t.astype(BF16)

    def local_part(h):
        gap = cum[h : h + 1, :] - cum_t[:, h : h + 1]
        decay = jnp.where(causal, jnp.exp(jnp.minimum(gap, 0.0)), 0.0)
        weighted = (nt(v_v[:, head(h)], g_v[:, head(h)]) * decay).astype(BF16)
        loc[0, h] = nn(k_b[head(h), :], weighted)
        loc[1, h] = nt(q_b[head(h), :], weighted)

    local_part(0)

    for h in range(nh):
        for i in range(1, nr):
            row_arrival(rec_a.at[h], ra_sem.at[h], i).wait_recv()
        run = jnp.zeros((part, width), F32)
        for p in range(nr):
            exc[h, 0, p] = run
            run = wgt[2, p, h : h + 1, :] * run + rec_a[h, p, 0].astype(F32)
        tot_b[h, 0] = run.astype(BF16)
        run = jnp.zeros((part, width), F32)
        for p in reversed(range(nr)):
            exc[h, 1, p] = run
            run = wgt[2, p, h : h + 1, :] * run + rec_a[h, p, 1].astype(F32)
        tot_b[h, 1] = run.astype(BF16)
        for i in range(1, ny):
            go(column_copy(tot_b.at[h, (y + i) // ny], rec_b.at[h, y], sb_sem.at[h, i - 1], rb_sem.at[h, y], i))
        rec_b[h, y] = jnp.zeros((part, width), BF16)

    lrec_b[y] = jnp.zeros((8, LANES), F32)
    for i in range(1, ny):
        column_arrival(lrec_b, rlb_sem, i).wait_recv()
    ahead = jnp.zeros((8, LANES), F32)
    for p in reversed(range(ny)):
        wgt_b[0, p] = jnp.where(p < y, jnp.exp(ahead), 0.0)
        ahead = ahead + jnp.where(p < y, lrec_b[p], 0.0)
    behind = jnp.zeros((8, LANES), F32)
    for p in range(ny):
        wgt_b[1, p] = jnp.where(p > y, jnp.exp(behind), 0.0)
        behind = behind + jnp.where(p > y, lrec_b[p], 0.0)

    for h in range(1, nh):
        local_part(h)
    g_t = flipped(g_v).astype(BF16)
    v_t = flipped(v_v).astype(BF16)

    for h in range(nh):
        for i in range(1, ny):
            column_arrival(rec_b.at[h], rb_sem.at[h], i).wait_recv()
        before = jnp.zeros((part, width), F32)
        after = jnp.zeros((part, width), F32)
        for p in range(ny):
            term = rec_b[h, p].astype(F32)
            before = before + wgt_b[0, p, h : h + 1, :] * term
            after = after + wgt_b[1, p, h : h + 1, :] * term
        for p in range(nr):
            buf_c[h, p, 0] = (wgt[0, p, h : h + 1, :] * before + exc[h, 0, p]).astype(BF16)
            buf_c[h, p, 1] = (wgt[1, p, h : h + 1, :] * after + exc[h, 1, p]).astype(BF16)
        for i in range(1, nr):
            go(row_copy(buf_c.at[h, (r + i) % nr], rec_c.at[h, r], sc_sem.at[h, i - 1], rc_sem.at[h, r], i))
        rec_c[h, r] = buf_c[h, r]

    for h in range(nh):
        for i in range(1, nr):
            row_arrival(rec_c.at[h], rc_sem.at[h], i).wait_recv()
        state = rec_c[h, :, 0].reshape(width, width)
        xt[head(h), :] = (loc[0, h] + nn(state, g_t[head(h), :]) * up_decay[h : h + 1, :]).astype(BF16)
        state = rec_c[h, :, 1].reshape(width, width)
        xt[head(nh + h), :] = (loc[1, h] + nn(state, v_t[head(h), :]) * down_decay[h : h + 1, :]).astype(BF16)

    loads[5].wait()
    loads[6].wait()

    def own(dest, pc):
        span_rows = pl.ds(pl.multiple_of(dest * chunk + pc * rows, rows), rows)
        return nn(wq_v[span_rows, :], xt[0:hw, :]) + nn(wk_v[span_rows, :], xt[hw : 2 * hw, :])

    def ring_copy(way, step, pc):
        at = pl.ds(pc * rows, rows)
        return pltpu.make_async_remote_copy(
            src_ref=sbuf.at[way, step, at],
            dst_ref=rbuf.at[way, step, at],
            send_sem=sz_sem.at[way, step, pc],
            recv_sem=rz_sem.at[way, step, pc],
            device_id={"head": (z + (1 if way == 0 else nz - 1)) % nz},
            device_id_type=MESH,
        )

    def relay(way, step, pc, fresh):
        away = half - step
        dest = (z + (away if way == 0 else nz - away)) % nz
        value = own(dest, pc)
        at = pl.ds(pc * rows, rows)
        if not fresh:
            ring_copy(way, step - 1, pc).wait_recv()
            value = value + rbuf[way, step - 1, at, :].astype(F32)
        sbuf[way, step, at, :] = value.astype(BF16)
        ring_copy(way, step, pc).start()

    mid = PIECES // 2
    for i in range(mid):
        relay(0, 0, i, True)
        relay(1, 0, mid + i, True)
    for i in range(mid):
        relay(0, 1, mid + i, True)
        relay(1, 1, i, True)
    for i in range(mid):
        relay(0, 1, i, False)
        relay(1, 1, mid + i, False)

    def ring_step(step, carry):
        for i in range(PIECES):
            relay(0, step, (mid + i) % PIECES, False)
            relay(1, step, i, False)
        return carry

    lax.fori_loop(2, half, ring_step, 0)
    for pc in range(PIECES):
        out_ref[pl.ds(pc * rows, rows), :] = own(z, pc)
    for i in range(PIECES):
        pc = i // 2 + mid * (i % 2)
        at = pl.ds(pc * rows, rows)
        for way in (i % 2, 1 - i % 2):
            ring_copy(1 - way, half - 1, pc).wait_recv()
            out_ref[at, :] += rbuf[1 - way, half - 1, at, :].astype(F32)

    for copy in sends:
        copy.wait_send()
    for way in range(2):
        for i in range(mid):
            ring_copy(way, 0, i + mid * way).wait_send()

    def drain(step, carry):
        for way in range(2):
            for pc in range(PIECES):
                ring_copy(way, step, pc).wait_send()
        return carry

    lax.fori_loop(1, half, drain, 0)


def shards(sizes, query_act, key_act, value_act, grad_output, log_decay, w_query, w_key):
    ny, nx, nc, nz = sizes
    span = query_act.shape[0]
    nh = log_decay.shape[1]
    width = query_act.shape[1] // nh
    hw = nh * width
    nr = nx * nc
    part = width // nr
    half = nz // 2
    features = w_query.shape[0]
    chunk = features // nz
    dims = (ny, nr, nc, nz, nh, span, chunk)
    vmem = pltpu.VMEM
    dma = pltpu.SemaphoreType.DMA
    scratch = [
        vmem((span, hw), BF16), vmem((span, hw), BF16), vmem((span, hw), BF16), vmem((span, hw), BF16),
        vmem((nh, span), F32), vmem((features, hw), BF16), vmem((features, hw), BF16),
        vmem((nh, nr, 2, part, width), BF16), vmem((nh, nr, 2, part, width), BF16),
        vmem((8, LANES), F32), vmem((nr, 8, LANES), F32),
        vmem((nh, 2, nr, part, width), F32), vmem((3, nr, 8, LANES), F32), vmem((2, ny, 8, LANES), F32),
        vmem((nh, 2, part, width), BF16), vmem((nh, ny, part, width), BF16),
        vmem((8, LANES), F32), vmem((ny, 8, LANES), F32),
        vmem((nh, nr, 2, part, width), BF16), vmem((nh, nr, 2, part, width), BF16),
        vmem((2, nh, width, span), F32), vmem((2 * hw, span), BF16),
        vmem((2, half, chunk, span), BF16), vmem((2, half, chunk, span), BF16),
        dma((7,)),
        dma((nh, nr - 1)), dma((nh, nr)), dma((nr - 1,)), dma((nr,)),
        dma((nh, ny - 1)), dma((nh, ny)), dma((ny - 1,)), dma((ny,)),
        dma((nh, nr - 1)), dma((nh, nr)),
        dma((2, half, PIECES)), dma((2, half, PIECES)),
    ]
    hbm = pl.BlockSpec(memory_space=pl.ANY)
    total = pl.pallas_call(
        functools.partial(kernel, dims),
        out_shape=pltpu.VMEM((chunk, span), F32),
        in_specs=[hbm] * 7,
        out_specs=pl.BlockSpec(memory_space=pltpu.VMEM),
        scratch_shapes=scratch,
        compiler_params=pltpu.CompilerParams(
            collective_id=0, has_side_effects=True, vmem_limit_bytes=56 * 1024 * 1024
        ),
        name="attention_backward",
    )(query_act, key_act, value_act, grad_output, log_decay.T, w_query, w_key)
    return total.astype(BF16)


def build(torus):
    sizes = tuple(torus.shape[a] for a in SEQ + ("head",))
    return jax.shard_map(
        functools.partial(shards, sizes),
        mesh=torus,
        in_specs=(
            P(SEQ, "head"),
            P(SEQ, "head"),
            P(SEQ, "head"),
            P(SEQ, "head"),
            P(SEQ, "head"),
            P(None, "head"),
            P(None, "head"),
        ),
        out_specs=P("head", SEQ),
        check_vma=False,
    )


def solution(mesh):
    torus = Mesh(
        mesh.devices.reshape(8, 4, 2, mesh.shape["head"]), ("seq_0", "seq_1", "seq_2", "head")
    )
    return build(torus)
```

```python
import functools

import jax
import jax.numpy as jnp
from jax import lax
from jax.experimental import pallas as pl
from jax.experimental.pallas import tpu as pltpu
from jax.sharding import Mesh
from jax.sharding import PartitionSpec as P

SEQ = ("seq_0", "seq_1", "seq_2")
F32 = jnp.float32
BF16 = jnp.bfloat16
MESH = pl.DeviceIdType.MESH
LANES = 128
PIECES = 2


def nn(a, b):
    return lax.dot_general(a, b, (((1,), (0,)), ((), ())), preferred_element_type=F32)


def nt(a, b):
    return lax.dot_general(a, b, (((1,), (1,)), ((), ())), preferred_element_type=F32)


def far_first(n):
    return sorted(range(1, n), key=lambda i: abs(2 * i - n))


def kernel(
    dims,
    q_hbm, k_hbm, v_hbm, g_hbm, ld_hbm, wq_hbm, wk_hbm,
    out_ref,
    q_v, k_v, v_v, g_v, ld_v, wq_v, wk_v,
    buf_a, rec_a, lbuf_a, lrec_a,
    exc, wgt, wgt_b, tot_b, rec_b, lbuf_b, lrec_b,
    buf_c, rec_c,
    loc, xt, sbuf, rbuf,
    in_sem,
    sa_sem, ra_sem, sla_sem, rla_sem,
    sb_sem, rb_sem, slb_sem, rlb_sem,
    sc_sem, rc_sem,
    sz_sem, rz_sem,
):
    ny, nr, nc, nz, nh, span, chunk = dims
    width = LANES
    hw = nh * width
    part = width // nr
    half = nz // 2
    rows = chunk // PIECES
    y = lax.axis_index("seq_0")
    r = lax.axis_index("seq_1") * nc + lax.axis_index("seq_2")
    z = lax.axis_index("head")

    def row_peer(p):
        return {"seq_1": p // nc, "seq_2": p % nc}

    loads = []
    for i, (src, dst) in enumerate(
        ((ld_hbm, ld_v), (k_hbm, k_v), (v_hbm, v_v), (q_hbm, q_v), (g_hbm, g_v), (wq_hbm, wq_v), (wk_hbm, wk_v))
    ):
        load = pltpu.make_async_copy(src, dst, in_sem.at[i])
        loads.append(load)
    for load in loads[:5]:
        load.start()

    barrier = pltpu.get_barrier_semaphore()
    for i in far_first(ny):
        pl.semaphore_signal(barrier, inc=1, device_id={"seq_0": (y + i) % ny}, device_id_type=MESH)
    for i in far_first(nr):
        pl.semaphore_signal(barrier, inc=1, device_id=row_peer((r + i) % nr), device_id_type=MESH)
    for step in (1, nz - 1):
        pl.semaphore_signal(barrier, inc=1, device_id={"head": (z + step) % nz}, device_id_type=MESH)

    loads[0].wait()
    ld = jnp.concatenate([ld_v[...], jnp.zeros((8 - nh, span), F32)], axis=0)
    first = lax.broadcasted_iota(jnp.int32, (span, span), 0)
    second = lax.broadcasted_iota(jnp.int32, (span, span), 1)
    causal = first <= second
    cum = lax.dot_general(
        ld, causal.astype(F32), (((1,), (0,)), ((), ())), precision=lax.Precision.HIGHEST, preferred_element_type=F32
    )
    last = cum[:, span - 1 : span]
    lbuf_a[...] = jnp.broadcast_to(last, (8, LANES))
    up_decay = jnp.exp(cum)
    down_decay = jnp.exp(jnp.minimum(last - cum, 0.0))

    def row_copy(src, dst, ssem, rsem, i):
        return pltpu.make_async_remote_copy(
            src_ref=src, dst_ref=dst, send_sem=ssem, recv_sem=rsem,
            device_id=row_peer((r + i) % nr), device_id_type=MESH,
        )

    def column_copy(src, dst, ssem, rsem, i):
        return pltpu.make_async_remote_copy(
            src_ref=src, dst_ref=dst, send_sem=ssem, recv_sem=rsem,
            device_id={"seq_0": (y + i) % ny}, device_id_type=MESH,
        )

    def column_arrival(dst, rsem, i):
        frm = (y + i) % ny
        return pltpu.make_async_remote_copy(
            src_ref=dst.at[frm],
            dst_ref=dst.at[frm],
            send_sem=rsem.at[frm],
            recv_sem=rsem.at[frm],
            device_id={"seq_0": frm},
            device_id_type=MESH,
        )

    def row_arrival(dst, rsem, i):
        frm = (r + i) % nr
        return pltpu.make_async_remote_copy(
            src_ref=dst.at[frm],
            dst_ref=dst.at[frm],
            send_sem=rsem.at[frm],
            recv_sem=rsem.at[frm],
            device_id=row_peer(frm),
            device_id_type=MESH,
        )

    sends = []

    def go(copy):
        copy.start()
        sends.append(copy)

    def flipped(ref):
        return ref[...].astype(F32).T

    def head(h):
        return slice(h * width, (h + 1) * width)

    loads[1].wait()
    k_t = flipped(k_v)
    loads[2].wait()
    loads[3].wait()
    q_t = flipped(q_v)
    loads[4].wait()
    for load in loads[5:]:
        load.start()
    for h in range(nh):
        kw = (k_t[head(h), :] * down_decay[h : h + 1, :]).astype(BF16)
        qw = (q_t[head(h), :] * up_decay[h : h + 1, :]).astype(BF16)
        buf_a[h, :, 0] = nn(kw, v_v[:, head(h)]).astype(BF16).reshape(nr, part, width)
        buf_a[h, :, 1] = nn(qw, g_v[:, head(h)]).astype(BF16).reshape(nr, part, width)

    pl.semaphore_wait(barrier, nr + ny)
    for i in far_first(nr):
        go(row_copy(lbuf_a, lrec_a.at[r], sla_sem.at[i - 1], rla_sem.at[r], i))
    lrec_a[r] = lbuf_a[...]
    for h in range(nh):
        for i in far_first(nr):
            go(row_copy(buf_a.at[h, (r + i) % nr], rec_a.at[h, r], sa_sem.at[h, i - 1], ra_sem.at[h, r], i))
        rec_a[h, r] = buf_a[h, r]

    for i in range(1, nr):
        row_arrival(lrec_a, rla_sem, i).wait_recv()
    ahead = jnp.zeros((8, LANES), F32)
    for p in range(nr):
        wgt[0, p] = jnp.exp(ahead)
        wgt[2, p] = jnp.exp(lrec_a[p])
        ahead = ahead + lrec_a[p]
    lbuf_b[...] = ahead
    for i in far_first(ny):
        go(column_copy(lbuf_b, lrec_b.at[y], slb_sem.at[i - 1], rlb_sem.at[y], i))
    behind = jnp.zeros((8, LANES), F32)
    for p in reversed(range(nr)):
        wgt[1, p] = jnp.exp(behind)
        behind = behind + lrec_a[p]

    cum_t = cum.T
    k_b = k_t.astype(BF16)
    q_b = q_t.astype(BF16)

    def local_part(h):
        gap = cum[h : h + 1, :] - cum_t[:, h : h + 1]
        decay = jnp.where(causal, jnp.exp(jnp.minimum(gap, 0.0)), 0.0)
        weighted = (nt(v_v[:, head(h)], g_v[:, head(h)]) * decay).astype(BF16)
        loc[0, h] = nn(k_b[head(h), :], weighted)
        loc[1, h] = nt(q_b[head(h), :], weighted)

    local_part(0)

    for h in range(nh):
        for i in range(1, nr):
            row_arrival(rec_a.at[h], ra_sem.at[h], i).wait_recv()
        run = jnp.zeros((part, width), F32)
        for p in range(nr):
            exc[h, 0, p] = run
            run = wgt[2, p, h : h + 1, :] * run + rec_a[h, p, 0].astype(F32)
        tot_b[h, 0] = run.astype(BF16)
        run = jnp.zeros((part, width), F32)
        for p in reversed(range(nr)):
            exc[h, 1, p] = run
            run = wgt[2, p, h : h + 1, :] * run + rec_a[h, p, 1].astype(F32)
        tot_b[h, 1] = run.astype(BF16)
        for i in far_first(ny):
            go(column_copy(tot_b.at[h, (y + i) // ny], rec_b.at[h, y], sb_sem.at[h, i - 1], rb_sem.at[h, y], i))
        rec_b[h, y] = jnp.zeros((part, width), BF16)

    for h in range(1, nh):
        local_part(h)
    g_t = flipped(g_v).astype(BF16)
    v_t = flipped(v_v).astype(BF16)

    lrec_b[y] = jnp.zeros((8, LANES), F32)
    for i in range(1, ny):
        column_arrival(lrec_b, rlb_sem, i).wait_recv()
    ahead = jnp.zeros((8, LANES), F32)
    for p in reversed(range(ny)):
        wgt_b[0, p] = jnp.where(p < y, jnp.exp(ahead), 0.0)
        ahead = ahead + jnp.where(p < y, lrec_b[p], 0.0)
    behind = jnp.zeros((8, LANES), F32)
    for p in range(ny):
        wgt_b[1, p] = jnp.where(p > y, jnp.exp(behind), 0.0)
        behind = behind + jnp.where(p > y, lrec_b[p], 0.0)

    for h in range(nh):
        for i in range(1, ny):
            column_arrival(rec_b.at[h], rb_sem.at[h], i).wait_recv()
        before = jnp.zeros((part, width), F32)
        after = jnp.zeros((part, width), F32)
        for p in range(ny):
            term = rec_b[h, p].astype(F32)
            before = before + wgt_b[0, p, h : h + 1, :] * term
            after = after + wgt_b[1, p, h : h + 1, :] * term
        for p in range(nr):
            buf_c[h, p, 0] = (wgt[0, p, h : h + 1, :] * before + exc[h, 0, p]).astype(BF16)
            buf_c[h, p, 1] = (wgt[1, p, h : h + 1, :] * after + exc[h, 1, p]).astype(BF16)
        for i in far_first(nr):
            go(row_copy(buf_c.at[h, (r + i) % nr], rec_c.at[h, r], sc_sem.at[h, i - 1], rc_sem.at[h, r], i))
        rec_c[h, r] = buf_c[h, r]

    for h in range(nh):
        for i in range(1, nr):
            row_arrival(rec_c.at[h], rc_sem.at[h], i).wait_recv()
        state = rec_c[h, :, 0].reshape(width, width)
        xt[head(h), :] = (loc[0, h] + nn(state, g_t[head(h), :]) * up_decay[h : h + 1, :]).astype(BF16)
        state = rec_c[h, :, 1].reshape(width, width)
        xt[head(nh + h), :] = (loc[1, h] + nn(state, v_t[head(h), :]) * down_decay[h : h + 1, :]).astype(BF16)

    loads[5].wait()
    loads[6].wait()

    def own(dest, pc):
        span_rows = pl.ds(pl.multiple_of(dest * chunk + pc * rows, rows), rows)
        return nn(wq_v[span_rows, :], xt[0:hw, :]) + nn(wk_v[span_rows, :], xt[hw : 2 * hw, :])

    def ring_copy(way, step, pc):
        at = pl.ds(pc * rows, rows)
        return pltpu.make_async_remote_copy(
            src_ref=sbuf.at[way, step, at],
            dst_ref=rbuf.at[way, step, at],
            send_sem=sz_sem.at[way, step, pc],
            recv_sem=rz_sem.at[way, step, pc],
            device_id={"head": (z + (1 if way == 0 else nz - 1)) % nz},
            device_id_type=MESH,
        )

    def relay(way, step, pc, fresh):
        away = half - step
        dest = (z + (away if way == 0 else nz - away)) % nz
        value = own(dest, pc)
        at = pl.ds(pc * rows, rows)
        if not fresh:
            ring_copy(way, step - 1, pc).wait_recv()
            value = value + rbuf[way, step - 1, at, :].astype(F32)
        sbuf[way, step, at, :] = value.astype(BF16)
        ring_copy(way, step, pc).start()

    mid = PIECES // 2
    for i in range(mid):
        relay(0, 0, i, True)
        relay(1, 0, mid + i, True)
    for i in range(mid):
        relay(0, 1, mid + i, True)
        relay(1, 1, i, True)
    for i in range(mid):
        relay(0, 1, i, False)
        relay(1, 1, mid + i, False)

    def ring_step(step, carry):
        for i in range(PIECES):
            relay(0, step, (mid + i) % PIECES, False)
            relay(1, step, i, False)
        return carry

    lax.fori_loop(2, half, ring_step, 0)
    for pc in range(PIECES):
        out_ref[pl.ds(pc * rows, rows), :] = own(z, pc)
    for i in range(PIECES):
        pc = i // 2 + mid * (i % 2)
        at = pl.ds(pc * rows, rows)
        for way in (i % 2, 1 - i % 2):
            ring_copy(1 - way, half - 1, pc).wait_recv()
            out_ref[at, :] += rbuf[1 - way, half - 1, at, :].astype(F32)

    for copy in sends:
        copy.wait_send()
    for way in range(2):
        for i in range(mid):
            ring_copy(way, 0, i + mid * way).wait_send()

    def drain(step, carry):
        for way in range(2):
            for pc in range(PIECES):
                ring_copy(way, step, pc).wait_send()
        return carry

    lax.fori_loop(1, half, drain, 0)


def shards(sizes, query_act, key_act, value_act, grad_output, log_decay, w_query, w_key):
    ny, nx, nc, nz = sizes
    span = query_act.shape[0]
    nh = log_decay.shape[1]
    width = query_act.shape[1] // nh
    hw = nh * width
    nr = nx * nc
    part = width // nr
    half = nz // 2
    features = w_query.shape[0]
    chunk = features // nz
    dims = (ny, nr, nc, nz, nh, span, chunk)
    vmem = pltpu.VMEM
    dma = pltpu.SemaphoreType.DMA
    scratch = [
        vmem((span, hw), BF16), vmem((span, hw), BF16), vmem((span, hw), BF16), vmem((span, hw), BF16),
        vmem((nh, span), F32), vmem((features, hw), BF16), vmem((features, hw), BF16),
        vmem((nh, nr, 2, part, width), BF16), vmem((nh, nr, 2, part, width), BF16),
        vmem((8, LANES), F32), vmem((nr, 8, LANES), F32),
        vmem((nh, 2, nr, part, width), F32), vmem((3, nr, 8, LANES), F32), vmem((2, ny, 8, LANES), F32),
        vmem((nh, 2, part, width), BF16), vmem((nh, ny, part, width), BF16),
        vmem((8, LANES), F32), vmem((ny, 8, LANES), F32),
        vmem((nh, nr, 2, part, width), BF16), vmem((nh, nr, 2, part, width), BF16),
        vmem((2, nh, width, span), F32), vmem((2 * hw, span), BF16),
        vmem((2, half, chunk, span), BF16), vmem((2, half, chunk, span), BF16),
        dma((7,)),
        dma((nh, nr - 1)), dma((nh, nr)), dma((nr - 1,)), dma((nr,)),
        dma((nh, ny - 1)), dma((nh, ny)), dma((ny - 1,)), dma((ny,)),
        dma((nh, nr - 1)), dma((nh, nr)),
        dma((2, half, PIECES)), dma((2, half, PIECES)),
    ]
    hbm = pl.BlockSpec(memory_space=pl.ANY)
    total = pl.pallas_call(
        functools.partial(kernel, dims),
        out_shape=pltpu.VMEM((chunk, span), F32),
        in_specs=[hbm] * 7,
        out_specs=pl.BlockSpec(memory_space=pltpu.VMEM),
        scratch_shapes=scratch,
        compiler_params=pltpu.CompilerParams(
            collective_id=0, has_side_effects=True, vmem_limit_bytes=56 * 1024 * 1024
        ),
        name="attention_backward",
    )(query_act, key_act, value_act, grad_output, log_decay.T, w_query, w_key)
    return total.astype(BF16)


def build(torus):
    sizes = tuple(torus.shape[a] for a in SEQ + ("head",))
    return jax.shard_map(
        functools.partial(shards, sizes),
        mesh=torus,
        in_specs=(
            P(SEQ, "head"),
            P(SEQ, "head"),
            P(SEQ, "head"),
            P(SEQ, "head"),
            P(SEQ, "head"),
            P(None, "head"),
            P(None, "head"),
        ),
        out_specs=P("head", SEQ),
        check_vma=False,
    )


def solution(mesh):
    torus = Mesh(
        mesh.devices.reshape(8, 4, 2, mesh.shape["head"]), ("seq_0", "seq_1", "seq_2", "head")
    )
    return build(torus)
```

```python
import functools

import jax
import jax.numpy as jnp
from jax import lax
from jax.experimental import pallas as pl
from jax.experimental.pallas import tpu as pltpu
from jax.sharding import Mesh
from jax.sharding import PartitionSpec as P

SEQ = ("seq_0", "seq_1", "seq_2")
F32 = jnp.float32
BF16 = jnp.bfloat16
MESH = pl.DeviceIdType.MESH
LANES = 128
PIECES = 2


def nn(a, b):
    return lax.dot_general(a, b, (((1,), (0,)), ((), ())), preferred_element_type=F32)


def nt(a, b):
    return lax.dot_general(a, b, (((1,), (1,)), ((), ())), preferred_element_type=F32)


def far_first(n):
    return sorted(range(1, n), key=lambda i: abs(2 * i - n))


def kernel(
    dims,
    q_hbm, k_hbm, v_hbm, g_hbm, ld_hbm, wq_hbm, wk_hbm,
    out_ref,
    q_v, k_v, v_v, g_v, ld_v, wq_v, wk_v,
    buf_a, rec_a, lbuf_a, lrec_a,
    exc, wgt, wgt_b, tot_b, rec_b, lbuf_b, lrec_b,
    buf_c, rec_c,
    loc, xt, sbuf, rbuf,
    in_sem,
    sa_sem, ra_sem, sla_sem, rla_sem,
    sb_sem, rb_sem, slb_sem, rlb_sem,
    sc_sem, rc_sem,
    sz_sem, rz_sem,
):
    ny, nr, nc, nz, nh, span, chunk = dims
    width = LANES
    hw = nh * width
    part = width // nr
    half = nz // 2
    rows = chunk // PIECES
    y = lax.axis_index("seq_0")
    r = lax.axis_index("seq_1") * nc + lax.axis_index("seq_2")
    z = lax.axis_index("head")

    def row_peer(p):
        return {"seq_1": p // nc, "seq_2": p % nc}

    loads = []
    for i, (src, dst) in enumerate(
        ((ld_hbm, ld_v), (k_hbm, k_v), (v_hbm, v_v), (q_hbm, q_v), (g_hbm, g_v), (wq_hbm, wq_v), (wk_hbm, wk_v))
    ):
        load = pltpu.make_async_copy(src, dst, in_sem.at[i])
        loads.append(load)
    for load in loads[:5]:
        load.start()

    barrier = pltpu.get_barrier_semaphore()
    for i in far_first(ny):
        pl.semaphore_signal(barrier, inc=1, device_id={"seq_0": (y + i) % ny}, device_id_type=MESH)
    for i in far_first(nr):
        pl.semaphore_signal(barrier, inc=1, device_id=row_peer((r + i) % nr), device_id_type=MESH)
    for step in (1, nz - 1):
        pl.semaphore_signal(barrier, inc=1, device_id={"head": (z + step) % nz}, device_id_type=MESH)

    loads[0].wait()
    ld = jnp.concatenate([ld_v[...], jnp.zeros((8 - nh, span), F32)], axis=0)
    first = lax.broadcasted_iota(jnp.int32, (span, span), 0)
    second = lax.broadcasted_iota(jnp.int32, (span, span), 1)
    causal = first <= second
    cum = lax.dot_general(
        ld, causal.astype(F32), (((1,), (0,)), ((), ())), precision=lax.Precision.HIGHEST, preferred_element_type=F32
    )
    last = cum[:, span - 1 : span]
    lbuf_a[...] = jnp.broadcast_to(last, (8, LANES))
    up_decay = jnp.exp(cum)
    down_decay = jnp.exp(jnp.minimum(last - cum, 0.0))

    def row_copy(src, dst, ssem, rsem, i):
        return pltpu.make_async_remote_copy(
            src_ref=src, dst_ref=dst, send_sem=ssem, recv_sem=rsem,
            device_id=row_peer((r + i) % nr), device_id_type=MESH,
        )

    def column_copy(src, dst, ssem, rsem, i):
        return pltpu.make_async_remote_copy(
            src_ref=src, dst_ref=dst, send_sem=ssem, recv_sem=rsem,
            device_id={"seq_0": (y + i) % ny}, device_id_type=MESH,
        )

    def column_arrival(dst, rsem, i):
        frm = (y + i) % ny
        return pltpu.make_async_remote_copy(
            src_ref=dst.at[frm],
            dst_ref=dst.at[frm],
            send_sem=rsem.at[frm],
            recv_sem=rsem.at[frm],
            device_id={"seq_0": frm},
            device_id_type=MESH,
        )

    def row_arrival(dst, rsem, i):
        frm = (r + i) % nr
        return pltpu.make_async_remote_copy(
            src_ref=dst.at[frm],
            dst_ref=dst.at[frm],
            send_sem=rsem.at[frm],
            recv_sem=rsem.at[frm],
            device_id=row_peer(frm),
            device_id_type=MESH,
        )

    sends = []

    def go(copy):
        copy.start()
        sends.append(copy)

    def flipped(ref):
        return ref[...].astype(F32).T

    def head(h):
        return slice(h * width, (h + 1) * width)

    loads[1].wait()
    k_t = flipped(k_v)
    loads[2].wait()
    loads[3].wait()
    q_t = flipped(q_v)
    loads[4].wait()
    for load in loads[5:]:
        load.start()
    for h in range(nh):
        kw = (k_t[head(h), :] * down_decay[h : h + 1, :]).astype(BF16)
        qw = (q_t[head(h), :] * up_decay[h : h + 1, :]).astype(BF16)
        buf_a[h, :, 0] = nn(kw, v_v[:, head(h)]).astype(BF16).reshape(nr, part, width)
        buf_a[h, :, 1] = nn(qw, g_v[:, head(h)]).astype(BF16).reshape(nr, part, width)

    pl.semaphore_wait(barrier, nr + ny)
    for i in far_first(nr):
        go(row_copy(lbuf_a, lrec_a.at[r], sla_sem.at[i - 1], rla_sem.at[r], i))
    lrec_a[r] = lbuf_a[...]
    for h in range(nh):
        for i in far_first(nr):
            go(row_copy(buf_a.at[h, (r + i) % nr], rec_a.at[h, r], sa_sem.at[h, i - 1], ra_sem.at[h, r], i))
        rec_a[h, r] = buf_a[h, r]

    for i in range(1, nr):
        row_arrival(lrec_a, rla_sem, i).wait_recv()
    ahead = jnp.zeros((8, LANES), F32)
    for p in range(nr):
        wgt[0, p] = jnp.exp(ahead)
        wgt[2, p] = jnp.exp(lrec_a[p])
        ahead = ahead + lrec_a[p]
    lbuf_b[...] = ahead
    for i in far_first(ny):
        go(column_copy(lbuf_b, lrec_b.at[y], slb_sem.at[i - 1], rlb_sem.at[y], i))
    behind = jnp.zeros((8, LANES), F32)
    for p in reversed(range(nr)):
        wgt[1, p] = jnp.exp(behind)
        behind = behind + lrec_a[p]

    cum_t = cum.T
    k_b = k_t.astype(BF16)
    q_b = q_t.astype(BF16)

    def local_part(h):
        gap = cum[h : h + 1, :] - cum_t[:, h : h + 1]
        decay = jnp.where(causal, jnp.exp(jnp.minimum(gap, 0.0)), 0.0)
        weighted = (nt(v_v[:, head(h)], g_v[:, head(h)]) * decay).astype(BF16)
        loc[0, h] = nn(k_b[head(h), :], weighted)
        loc[1, h] = nt(q_b[head(h), :], weighted)

    local_part(0)

    for h in range(nh):
        for i in range(1, nr):
            row_arrival(rec_a.at[h], ra_sem.at[h], i).wait_recv()
        run = jnp.zeros((part, width), F32)
        for p in range(nr):
            exc[h, 0, p] = run
            run = wgt[2, p, h : h + 1, :] * run + rec_a[h, p, 0].astype(F32)
        tot_b[h, 0] = run.astype(BF16)
        run = jnp.zeros((part, width), F32)
        for p in reversed(range(nr)):
            exc[h, 1, p] = run
            run = wgt[2, p, h : h + 1, :] * run + rec_a[h, p, 1].astype(F32)
        tot_b[h, 1] = run.astype(BF16)
        for i in far_first(ny):
            go(column_copy(tot_b.at[h, (y + i) // ny], rec_b.at[h, y], sb_sem.at[h, i - 1], rb_sem.at[h, y], i))
        rec_b[h, y] = jnp.zeros((part, width), BF16)

    for h in range(1, nh):
        local_part(h)
    g_t = flipped(g_v).astype(BF16)
    v_t = flipped(v_v).astype(BF16)

    lrec_b[y] = jnp.zeros((8, LANES), F32)
    for i in range(1, ny):
        column_arrival(lrec_b, rlb_sem, i).wait_recv()
    ahead = jnp.zeros((8, LANES), F32)
    for p in reversed(range(ny)):
        wgt_b[0, p] = jnp.where(p < y, jnp.exp(ahead), 0.0)
        ahead = ahead + jnp.where(p < y, lrec_b[p], 0.0)
    behind = jnp.zeros((8, LANES), F32)
    for p in range(ny):
        wgt_b[1, p] = jnp.where(p > y, jnp.exp(behind), 0.0)
        behind = behind + jnp.where(p > y, lrec_b[p], 0.0)

    for h in range(nh):
        for i in range(1, ny):
            column_arrival(rec_b.at[h], rb_sem.at[h], i).wait_recv()
        before = jnp.zeros((part, width), F32)
        after = jnp.zeros((part, width), F32)
        for p in range(ny):
            term = rec_b[h, p].astype(F32)
            before = before + wgt_b[0, p, h : h + 1, :] * term
            after = after + wgt_b[1, p, h : h + 1, :] * term
        for p in range(nr):
            buf_c[h, p, 0] = (wgt[0, p, h : h + 1, :] * before + exc[h, 0, p]).astype(BF16)
            buf_c[h, p, 1] = (wgt[1, p, h : h + 1, :] * after + exc[h, 1, p]).astype(BF16)
        for i in far_first(nr):
            go(row_copy(buf_c.at[h, (r + i) % nr], rec_c.at[h, r], sc_sem.at[h, i - 1], rc_sem.at[h, r], i))
        rec_c[h, r] = buf_c[h, r]

    def finish(h):
        for i in range(1, nr):
            row_arrival(rec_c.at[h], rc_sem.at[h], i).wait_recv()
        state = rec_c[h, :, 0].reshape(width, width)
        xt[head(h), :] = (loc[0, h] + nn(state, g_t[head(h), :]) * up_decay[h : h + 1, :]).astype(BF16)
        state = rec_c[h, :, 1].reshape(width, width)
        xt[head(nh + h), :] = (loc[1, h] + nn(state, v_t[head(h), :]) * down_decay[h : h + 1, :]).astype(BF16)

    mid = PIECES // 2
    most = (nh - 1) * width
    far = (z + half) % nz

    def some(pc, lo, hi):
        span_rows = pl.ds(pl.multiple_of(far * chunk + pc * rows, rows), rows)
        return nn(wq_v[span_rows, lo:hi], xt[lo:hi, :]) + nn(wk_v[span_rows, lo:hi], xt[hw + lo : hw + hi, :])

    for h in range(nh - 1):
        finish(h)
    loads[5].wait()
    loads[6].wait()
    for pc in range(PIECES):
        out_ref[pl.ds(pc * rows, rows), :] = some(pc, 0, most)
    finish(nh - 1)

    def own(dest, pc):
        span_rows = pl.ds(pl.multiple_of(dest * chunk + pc * rows, rows), rows)
        return nn(wq_v[span_rows, :], xt[0:hw, :]) + nn(wk_v[span_rows, :], xt[hw : 2 * hw, :])

    def ring_copy(way, step, pc):
        at = pl.ds(pc * rows, rows)
        return pltpu.make_async_remote_copy(
            src_ref=sbuf.at[way, step, at],
            dst_ref=rbuf.at[way, step, at],
            send_sem=sz_sem.at[way, step, pc],
            recv_sem=rz_sem.at[way, step, pc],
            device_id={"head": (z + (1 if way == 0 else nz - 1)) % nz},
            device_id_type=MESH,
        )

    def relay(way, step, pc, fresh):
        away = half - step
        dest = (z + (away if way == 0 else nz - away)) % nz
        value = own(dest, pc)
        at = pl.ds(pc * rows, rows)
        if not fresh:
            ring_copy(way, step - 1, pc).wait_recv()
            value = value + rbuf[way, step - 1, at, :].astype(F32)
        sbuf[way, step, at, :] = value.astype(BF16)
        ring_copy(way, step, pc).start()

    for i in range(mid):
        for way in range(2):
            pc = mid * way + i
            at = pl.ds(pc * rows, rows)
            sbuf[way, 0, at, :] = (out_ref[at, :] + some(pc, most, hw)).astype(BF16)
            ring_copy(way, 0, pc).start()
    for i in range(mid):
        relay(0, 1, mid + i, True)
        relay(1, 1, i, True)
    for i in range(mid):
        relay(0, 1, i, False)
        relay(1, 1, mid + i, False)

    def ring_step(step, carry):
        for i in range(PIECES):
            relay(0, step, (mid + i) % PIECES, False)
            relay(1, step, i, False)
        return carry

    lax.fori_loop(2, half, ring_step, 0)
    for pc in range(PIECES):
        out_ref[pl.ds(pc * rows, rows), :] = own(z, pc)
    for copy in sends:
        copy.wait_send()
    for way in range(2):
        for i in range(mid):
            ring_copy(way, 0, i + mid * way).wait_send()

    def drain(step, carry):
        for way in range(2):
            for pc in range(PIECES):
                ring_copy(way, step, pc).wait_send()
        return carry

    lax.fori_loop(1, half - 1, drain, 0)
    for i in range(PIECES):
        pc = i // 2 + mid * (i % 2)
        at = pl.ds(pc * rows, rows)
        for way in (i % 2, 1 - i % 2):
            ring_copy(1 - way, half - 1, pc).wait_recv()
            out_ref[at, :] += rbuf[1 - way, half - 1, at, :].astype(F32)

    for way in range(2):
        for pc in range(PIECES):
            ring_copy(way, half - 1, pc).wait_send()


def shards(sizes, query_act, key_act, value_act, grad_output, log_decay, w_query, w_key):
    ny, nx, nc, nz = sizes
    span = query_act.shape[0]
    nh = log_decay.shape[1]
    width = query_act.shape[1] // nh
    hw = nh * width
    nr = nx * nc
    part = width // nr
    half = nz // 2
    features = w_query.shape[0]
    chunk = features // nz
    dims = (ny, nr, nc, nz, nh, span, chunk)
    vmem = pltpu.VMEM
    dma = pltpu.SemaphoreType.DMA
    scratch = [
        vmem((span, hw), BF16), vmem((span, hw), BF16), vmem((span, hw), BF16), vmem((span, hw), BF16),
        vmem((nh, span), F32), vmem((features, hw), BF16), vmem((features, hw), BF16),
        vmem((nh, nr, 2, part, width), BF16), vmem((nh, nr, 2, part, width), BF16),
        vmem((8, LANES), F32), vmem((nr, 8, LANES), F32),
        vmem((nh, 2, nr, part, width), F32), vmem((3, nr, 8, LANES), F32), vmem((2, ny, 8, LANES), F32),
        vmem((nh, 2, part, width), BF16), vmem((nh, ny, part, width), BF16),
        vmem((8, LANES), F32), vmem((ny, 8, LANES), F32),
        vmem((nh, nr, 2, part, width), BF16), vmem((nh, nr, 2, part, width), BF16),
        vmem((2, nh, width, span), F32), vmem((2 * hw, span), BF16),
        vmem((2, half, chunk, span), BF16), vmem((2, half, chunk, span), BF16),
        dma((7,)),
        dma((nh, nr - 1)), dma((nh, nr)), dma((nr - 1,)), dma((nr,)),
        dma((nh, ny - 1)), dma((nh, ny)), dma((ny - 1,)), dma((ny,)),
        dma((nh, nr - 1)), dma((nh, nr)),
        dma((2, half, PIECES)), dma((2, half, PIECES)),
    ]
    hbm = pl.BlockSpec(memory_space=pl.ANY)
    total = pl.pallas_call(
        functools.partial(kernel, dims),
        out_shape=pltpu.VMEM((chunk, span), F32),
        in_specs=[hbm] * 7,
        out_specs=pl.BlockSpec(memory_space=pltpu.VMEM),
        scratch_shapes=scratch,
        compiler_params=pltpu.CompilerParams(
            collective_id=0, has_side_effects=True, vmem_limit_bytes=56 * 1024 * 1024
        ),
        name="attention_backward",
    )(query_act, key_act, value_act, grad_output, log_decay.T, w_query, w_key)
    return total.astype(BF16)


def build(torus):
    sizes = tuple(torus.shape[a] for a in SEQ + ("head",))
    return jax.shard_map(
        functools.partial(shards, sizes),
        mesh=torus,
        in_specs=(
            P(SEQ, "head"),
            P(SEQ, "head"),
            P(SEQ, "head"),
            P(SEQ, "head"),
            P(SEQ, "head"),
            P(None, "head"),
            P(None, "head"),
        ),
        out_specs=P("head", SEQ),
        check_vma=False,
    )


def solution(mesh):
    torus = Mesh(
        mesh.devices.reshape(8, 4, 2, mesh.shape["head"]), ("seq_0", "seq_1", "seq_2", "head")
    )
    return build(torus)
```

```python
import functools

import jax
import jax.numpy as jnp
from jax import lax
from jax.experimental import pallas as pl
from jax.experimental.pallas import tpu as pltpu
from jax.sharding import Mesh
from jax.sharding import PartitionSpec as P

SEQ = ("seq_0", "seq_1", "seq_2")
F32 = jnp.float32
BF16 = jnp.bfloat16
MESH = pl.DeviceIdType.MESH
LANES = 128
PIECES = 2


def nn(a, b):
    return lax.dot_general(a, b, (((1,), (0,)), ((), ())), preferred_element_type=F32)


def nt(a, b):
    return lax.dot_general(a, b, (((1,), (1,)), ((), ())), preferred_element_type=F32)


def far_first(n):
    return sorted(range(1, n), key=lambda i: abs(2 * i - n))


def kernel(
    dims,
    q_hbm, k_hbm, v_hbm, g_hbm, ld_hbm, wq_hbm, wk_hbm,
    out_ref,
    q_v, k_v, v_v, g_v, ld_v, wq_v, wk_v,
    buf_a, rec_a, lbuf_a, lrec_a,
    exc, wgt, wgt_b, tot_b, rec_b, lbuf_b, lrec_b,
    buf_c, rec_c,
    loc, xt, sbuf, rbuf,
    in_sem,
    sa_sem, ra_sem, sla_sem, rla_sem,
    sb_sem, rb_sem, slb_sem, rlb_sem,
    sc_sem, rc_sem,
    sz_sem, rz_sem,
):
    ny, nr, nc, nz, nh, span, chunk = dims
    width = LANES
    hw = nh * width
    part = width // nr
    half = nz // 2
    rows = chunk // PIECES
    y = lax.axis_index("seq_0")
    r = lax.axis_index("seq_1") * nc + lax.axis_index("seq_2")
    z = lax.axis_index("head")

    def row_peer(p):
        return {"seq_1": p // nc, "seq_2": p % nc}

    loads = []
    for i, (src, dst) in enumerate(
        ((ld_hbm, ld_v), (k_hbm, k_v), (v_hbm, v_v), (q_hbm, q_v), (g_hbm, g_v), (wq_hbm, wq_v), (wk_hbm, wk_v))
    ):
        load = pltpu.make_async_copy(src, dst, in_sem.at[i])
        loads.append(load)
    for load in loads[:5]:
        load.start()

    barrier = pltpu.get_barrier_semaphore()
    for i in far_first(ny):
        pl.semaphore_signal(barrier, inc=1, device_id={"seq_0": (y + i) % ny}, device_id_type=MESH)
    for i in far_first(nr):
        pl.semaphore_signal(barrier, inc=1, device_id=row_peer((r + i) % nr), device_id_type=MESH)
    for step in (1, nz - 1):
        pl.semaphore_signal(barrier, inc=1, device_id={"head": (z + step) % nz}, device_id_type=MESH)

    loads[0].wait()
    ld = jnp.concatenate([ld_v[...], jnp.zeros((8 - nh, span), F32)], axis=0)
    first = lax.broadcasted_iota(jnp.int32, (span, span), 0)
    second = lax.broadcasted_iota(jnp.int32, (span, span), 1)
    causal = first <= second
    cum = lax.dot_general(
        ld, causal.astype(F32), (((1,), (0,)), ((), ())), precision=lax.Precision.HIGHEST, preferred_element_type=F32
    )
    last = cum[:, span - 1 : span]
    lbuf_a[...] = jnp.broadcast_to(last, (8, LANES))
    up_decay = jnp.exp(cum)
    down_decay = jnp.exp(jnp.minimum(last - cum, 0.0))

    def row_copy(src, dst, ssem, rsem, i):
        return pltpu.make_async_remote_copy(
            src_ref=src, dst_ref=dst, send_sem=ssem, recv_sem=rsem,
            device_id=row_peer((r + i) % nr), device_id_type=MESH,
        )

    def column_copy(src, dst, ssem, rsem, i):
        return pltpu.make_async_remote_copy(
            src_ref=src, dst_ref=dst, send_sem=ssem, recv_sem=rsem,
            device_id={"seq_0": (y + i) % ny}, device_id_type=MESH,
        )

    def column_arrival(dst, rsem, i):
        frm = (y + i) % ny
        return pltpu.make_async_remote_copy(
            src_ref=dst.at[frm],
            dst_ref=dst.at[frm],
            send_sem=rsem.at[frm],
            recv_sem=rsem.at[frm],
            device_id={"seq_0": frm},
            device_id_type=MESH,
        )

    def row_arrival(dst, rsem, i):
        frm = (r + i) % nr
        return pltpu.make_async_remote_copy(
            src_ref=dst.at[frm],
            dst_ref=dst.at[frm],
            send_sem=rsem.at[frm],
            recv_sem=rsem.at[frm],
            device_id=row_peer(frm),
            device_id_type=MESH,
        )

    sends = []

    def go(copy):
        copy.start()
        sends.append(copy)

    def flipped(ref):
        return ref[...].T

    def head(h):
        return slice(h * width, (h + 1) * width)

    loads[1].wait()
    k_t = flipped(k_v)
    loads[2].wait()
    loads[3].wait()
    q_t = flipped(q_v)
    loads[4].wait()
    for load in loads[5:]:
        load.start()
    for h in range(nh):
        kw = (k_t[head(h), :].astype(F32) * down_decay[h : h + 1, :]).astype(BF16)
        qw = (q_t[head(h), :].astype(F32) * up_decay[h : h + 1, :]).astype(BF16)
        buf_a[h, :, 0] = nn(kw, v_v[:, head(h)]).astype(BF16).reshape(nr, part, width)
        buf_a[h, :, 1] = nn(qw, g_v[:, head(h)]).astype(BF16).reshape(nr, part, width)

    pl.semaphore_wait(barrier, nr + ny)
    for i in far_first(nr):
        go(row_copy(lbuf_a, lrec_a.at[r], sla_sem.at[i - 1], rla_sem.at[r], i))
    lrec_a[r] = lbuf_a[...]
    for h in range(nh):
        for i in far_first(nr):
            go(row_copy(buf_a.at[h, (r + i) % nr], rec_a.at[h, r], sa_sem.at[h, i - 1], ra_sem.at[h, r], i))
        rec_a[h, r] = buf_a[h, r]

    for i in range(1, nr):
        row_arrival(lrec_a, rla_sem, i).wait_recv()
    ahead = jnp.zeros((8, LANES), F32)
    for p in range(nr):
        wgt[0, p] = jnp.exp(ahead)
        wgt[2, p] = jnp.exp(lrec_a[p])
        ahead = ahead + lrec_a[p]
    lbuf_b[...] = ahead
    for i in far_first(ny):
        go(column_copy(lbuf_b, lrec_b.at[y], slb_sem.at[i - 1], rlb_sem.at[y], i))
    behind = jnp.zeros((8, LANES), F32)
    for p in reversed(range(nr)):
        wgt[1, p] = jnp.exp(behind)
        behind = behind + lrec_a[p]

    cum_t = cum.T

    def local_part(h):
        gap = cum[h : h + 1, :] - cum_t[:, h : h + 1]
        decay = jnp.where(causal, jnp.exp(jnp.minimum(gap, 0.0)), 0.0)
        weighted = (nt(v_v[:, head(h)], g_v[:, head(h)]) * decay).astype(BF16)
        loc[0, h] = nn(k_t[head(h), :], weighted)
        loc[1, h] = nt(q_t[head(h), :], weighted)

    local_part(0)

    for h in range(nh):
        for i in range(1, nr):
            row_arrival(rec_a.at[h], ra_sem.at[h], i).wait_recv()
        run = jnp.zeros((part, width), F32)
        for p in range(nr):
            exc[h, 0, p] = run
            run = wgt[2, p, h : h + 1, :] * run + rec_a[h, p, 0].astype(F32)
        tot_b[h, 0] = run.astype(BF16)
        run = jnp.zeros((part, width), F32)
        for p in reversed(range(nr)):
            exc[h, 1, p] = run
            run = wgt[2, p, h : h + 1, :] * run + rec_a[h, p, 1].astype(F32)
        tot_b[h, 1] = run.astype(BF16)
        for i in far_first(ny):
            go(column_copy(tot_b.at[h, (y + i) // ny], rec_b.at[h, y], sb_sem.at[h, i - 1], rb_sem.at[h, y], i))
        rec_b[h, y] = jnp.zeros((part, width), BF16)

    for h in range(1, nh):
        local_part(h)
    g_t = flipped(g_v)
    v_t = flipped(v_v)

    lrec_b[y] = jnp.zeros((8, LANES), F32)
    for i in range(1, ny):
        column_arrival(lrec_b, rlb_sem, i).wait_recv()
    ahead = jnp.zeros((8, LANES), F32)
    for p in reversed(range(ny)):
        wgt_b[0, p] = jnp.where(p < y, jnp.exp(ahead), 0.0)
        ahead = ahead + jnp.where(p < y, lrec_b[p], 0.0)
    behind = jnp.zeros((8, LANES), F32)
    for p in range(ny):
        wgt_b[1, p] = jnp.where(p > y, jnp.exp(behind), 0.0)
        behind = behind + jnp.where(p > y, lrec_b[p], 0.0)

    for h in range(nh):
        for i in range(1, ny):
            column_arrival(rec_b.at[h], rb_sem.at[h], i).wait_recv()
        before = jnp.zeros((part, width), F32)
        after = jnp.zeros((part, width), F32)
        for p in range(ny):
            term = rec_b[h, p].astype(F32)
            before = before + wgt_b[0, p, h : h + 1, :] * term
            after = after + wgt_b[1, p, h : h + 1, :] * term
        for p in range(nr):
            buf_c[h, p, 0] = (wgt[0, p, h : h + 1, :] * before + exc[h, 0, p]).astype(BF16)
            buf_c[h, p, 1] = (wgt[1, p, h : h + 1, :] * after + exc[h, 1, p]).astype(BF16)
        for i in far_first(nr):
            go(row_copy(buf_c.at[h, (r + i) % nr], rec_c.at[h, r], sc_sem.at[h, i - 1], rc_sem.at[h, r], i))
        rec_c[h, r] = buf_c[h, r]

    def finish(h):
        for i in range(1, nr):
            row_arrival(rec_c.at[h], rc_sem.at[h], i).wait_recv()
        state = rec_c[h, :, 0].reshape(width, width)
        xt[head(h), :] = (loc[0, h] + nn(state, g_t[head(h), :]) * up_decay[h : h + 1, :]).astype(BF16)
        state = rec_c[h, :, 1].reshape(width, width)
        xt[head(nh + h), :] = (loc[1, h] + nn(state, v_t[head(h), :]) * down_decay[h : h + 1, :]).astype(BF16)

    mid = PIECES // 2
    most = (nh - 1) * width
    far = (z + half) % nz

    def some(pc, lo, hi):
        span_rows = pl.ds(pl.multiple_of(far * chunk + pc * rows, rows), rows)
        return nn(wq_v[span_rows, lo:hi], xt[lo:hi, :]) + nn(wk_v[span_rows, lo:hi], xt[hw + lo : hw + hi, :])

    for h in range(nh - 1):
        finish(h)
    loads[5].wait()
    loads[6].wait()
    for pc in range(PIECES):
        out_ref[pl.ds(pc * rows, rows), :] = some(pc, 0, most)
    finish(nh - 1)

    def own(dest, pc):
        span_rows = pl.ds(pl.multiple_of(dest * chunk + pc * rows, rows), rows)
        return nn(wq_v[span_rows, :], xt[0:hw, :]) + nn(wk_v[span_rows, :], xt[hw : 2 * hw, :])

    def ring_copy(way, step, pc):
        at = pl.ds(pc * rows, rows)
        return pltpu.make_async_remote_copy(
            src_ref=sbuf.at[way, step, at],
            dst_ref=rbuf.at[way, step, at],
            send_sem=sz_sem.at[way, step, pc],
            recv_sem=rz_sem.at[way, step, pc],
            device_id={"head": (z + (1 if way == 0 else nz - 1)) % nz},
            device_id_type=MESH,
        )

    def relay(way, step, pc, fresh):
        away = half - step
        dest = (z + (away if way == 0 else nz - away)) % nz
        value = own(dest, pc)
        at = pl.ds(pc * rows, rows)
        if not fresh:
            ring_copy(way, step - 1, pc).wait_recv()
            value = value + rbuf[way, step - 1, at, :].astype(F32)
        sbuf[way, step, at, :] = value.astype(BF16)
        ring_copy(way, step, pc).start()

    for i in range(mid):
        for way in range(2):
            pc = mid * way + i
            at = pl.ds(pc * rows, rows)
            sbuf[way, 0, at, :] = (out_ref[at, :] + some(pc, most, hw)).astype(BF16)
            ring_copy(way, 0, pc).start()
    for i in range(mid):
        relay(0, 1, mid + i, True)
        relay(1, 1, i, True)
    for i in range(mid):
        relay(0, 1, i, False)
        relay(1, 1, mid + i, False)

    def ring_step(step, carry):
        for i in range(PIECES):
            relay(0, step, (mid + i) % PIECES, False)
            relay(1, step, i, False)
        return carry

    lax.fori_loop(2, half, ring_step, 0)
    for pc in range(PIECES):
        out_ref[pl.ds(pc * rows, rows), :] = own(z, pc)
    for copy in sends:
        copy.wait_send()
    for way in range(2):
        for i in range(mid):
            ring_copy(way, 0, i + mid * way).wait_send()

    def drain(step, carry):
        for way in range(2):
            for pc in range(PIECES):
                ring_copy(way, step, pc).wait_send()
        return carry

    lax.fori_loop(1, half - 1, drain, 0)
    for i in range(PIECES):
        pc = i // 2 + mid * (i % 2)
        at = pl.ds(pc * rows, rows)
        for way in (i % 2, 1 - i % 2):
            ring_copy(1 - way, half - 1, pc).wait_recv()
            out_ref[at, :] += rbuf[1 - way, half - 1, at, :].astype(F32)

    for way in range(2):
        for pc in range(PIECES):
            ring_copy(way, half - 1, pc).wait_send()


def shards(sizes, query_act, key_act, value_act, grad_output, log_decay, w_query, w_key):
    ny, nx, nc, nz = sizes
    span = query_act.shape[0]
    nh = log_decay.shape[1]
    width = query_act.shape[1] // nh
    hw = nh * width
    nr = nx * nc
    part = width // nr
    half = nz // 2
    features = w_query.shape[0]
    chunk = features // nz
    dims = (ny, nr, nc, nz, nh, span, chunk)
    vmem = pltpu.VMEM
    dma = pltpu.SemaphoreType.DMA
    scratch = [
        vmem((span, hw), BF16), vmem((span, hw), BF16), vmem((span, hw), BF16), vmem((span, hw), BF16),
        vmem((nh, span), F32), vmem((features, hw), BF16), vmem((features, hw), BF16),
        vmem((nh, nr, 2, part, width), BF16), vmem((nh, nr, 2, part, width), BF16),
        vmem((8, LANES), F32), vmem((nr, 8, LANES), F32),
        vmem((nh, 2, nr, part, width), F32), vmem((3, nr, 8, LANES), F32), vmem((2, ny, 8, LANES), F32),
        vmem((nh, 2, part, width), BF16), vmem((nh, ny, part, width), BF16),
        vmem((8, LANES), F32), vmem((ny, 8, LANES), F32),
        vmem((nh, nr, 2, part, width), BF16), vmem((nh, nr, 2, part, width), BF16),
        vmem((2, nh, width, span), F32), vmem((2 * hw, span), BF16),
        vmem((2, half, chunk, span), BF16), vmem((2, half, chunk, span), BF16),
        dma((7,)),
        dma((nh, nr - 1)), dma((nh, nr)), dma((nr - 1,)), dma((nr,)),
        dma((nh, ny - 1)), dma((nh, ny)), dma((ny - 1,)), dma((ny,)),
        dma((nh, nr - 1)), dma((nh, nr)),
        dma((2, half, PIECES)), dma((2, half, PIECES)),
    ]
    hbm = pl.BlockSpec(memory_space=pl.ANY)
    total = pl.pallas_call(
        functools.partial(kernel, dims),
        out_shape=pltpu.VMEM((chunk, span), F32),
        in_specs=[hbm] * 7,
        out_specs=pl.BlockSpec(memory_space=pltpu.VMEM),
        scratch_shapes=scratch,
        compiler_params=pltpu.CompilerParams(
            collective_id=0, has_side_effects=True, vmem_limit_bytes=56 * 1024 * 1024
        ),
        name="attention_backward",
    )(query_act, key_act, value_act, grad_output, log_decay.T, w_query, w_key)
    return total.astype(BF16)


def build(torus):
    sizes = tuple(torus.shape[a] for a in SEQ + ("head",))
    return jax.shard_map(
        functools.partial(shards, sizes),
        mesh=torus,
        in_specs=(
            P(SEQ, "head"),
            P(SEQ, "head"),
            P(SEQ, "head"),
            P(SEQ, "head"),
            P(SEQ, "head"),
            P(None, "head"),
            P(None, "head"),
        ),
        out_specs=P("head", SEQ),
        check_vma=False,
    )


def solution(mesh):
    torus = Mesh(
        mesh.devices.reshape(8, 4, 2, mesh.shape["head"]), ("seq_0", "seq_1", "seq_2", "head")
    )
    return build(torus)
```

```python
import functools

import jax
import jax.numpy as jnp
from jax import lax
from jax.experimental import pallas as pl
from jax.experimental.pallas import tpu as pltpu
from jax.sharding import Mesh
from jax.sharding import PartitionSpec as P

SEQ = ("seq_0", "seq_1", "seq_2")
F32 = jnp.float32
BF16 = jnp.bfloat16
MESH = pl.DeviceIdType.MESH
LANES = 128
PIECES = 2


def nn(a, b):
    return lax.dot_general(a, b, (((1,), (0,)), ((), ())), preferred_element_type=F32)


def nt(a, b):
    return lax.dot_general(a, b, (((1,), (1,)), ((), ())), preferred_element_type=F32)


def far_first(n):
    return sorted(range(1, n), key=lambda i: abs(2 * i - n))


def kernel(
    dims,
    q_hbm, k_hbm, v_hbm, g_hbm, ld_hbm, wq_hbm, wk_hbm,
    out_ref,
    q_v, k_v, v_v, g_v, ld_v, wq_v, wk_v,
    buf_a, rec_a, lbuf_a, lrec_a,
    exc, wgt, wgt_b, tot_b, rec_b, lbuf_b, lrec_b,
    buf_c, rec_c,
    loc, xt, sbuf, rbuf,
    in_sem,
    sa_sem, ra_sem, sla_sem, rla_sem,
    sb_sem, rb_sem, slb_sem, rlb_sem,
    sc_sem, rc_sem,
    sz_sem, rz_sem,
):
    ny, nr, nc, nz, nh, span, chunk = dims
    width = LANES
    hw = nh * width
    part = width // nr
    half = nz // 2
    rows = chunk // PIECES
    y = lax.axis_index("seq_0")
    r = lax.axis_index("seq_1") * nc + lax.axis_index("seq_2")
    z = lax.axis_index("head")

    def row_peer(p):
        return {"seq_1": p // nc, "seq_2": p % nc}

    loads = []
    for i, (src, dst) in enumerate(
        ((ld_hbm, ld_v), (k_hbm, k_v), (v_hbm, v_v), (q_hbm, q_v), (g_hbm, g_v), (wq_hbm, wq_v), (wk_hbm, wk_v))
    ):
        load = pltpu.make_async_copy(src, dst, in_sem.at[i])
        loads.append(load)
    for load in loads[:5]:
        load.start()

    barrier = pltpu.get_barrier_semaphore()
    for i in far_first(ny):
        pl.semaphore_signal(barrier, inc=1, device_id={"seq_0": (y + i) % ny}, device_id_type=MESH)
    for i in far_first(nr):
        pl.semaphore_signal(barrier, inc=1, device_id=row_peer((r + i) % nr), device_id_type=MESH)
    for step in (1, nz - 1):
        pl.semaphore_signal(barrier, inc=1, device_id={"head": (z + step) % nz}, device_id_type=MESH)

    loads[0].wait()
    ld = jnp.concatenate([ld_v[...], jnp.zeros((8 - nh, span), F32)], axis=0)
    first = lax.broadcasted_iota(jnp.int32, (span, span), 0)
    second = lax.broadcasted_iota(jnp.int32, (span, span), 1)
    causal = first <= second
    cum = lax.dot_general(
        ld, causal.astype(F32), (((1,), (0,)), ((), ())), precision=lax.Precision.HIGHEST, preferred_element_type=F32
    )
    last = cum[:, span - 1 : span]
    lbuf_a[...] = jnp.broadcast_to(last, (8, LANES))
    up_decay = jnp.exp(cum)
    down_decay = jnp.exp(jnp.minimum(last - cum, 0.0))

    def row_copy(src, dst, ssem, rsem, i):
        return pltpu.make_async_remote_copy(
            src_ref=src, dst_ref=dst, send_sem=ssem, recv_sem=rsem,
            device_id=row_peer((r + i) % nr), device_id_type=MESH,
        )

    def column_copy(src, dst, ssem, rsem, i):
        return pltpu.make_async_remote_copy(
            src_ref=src, dst_ref=dst, send_sem=ssem, recv_sem=rsem,
            device_id={"seq_0": (y + i) % ny}, device_id_type=MESH,
        )

    def column_arrival(dst, rsem, i):
        frm = (y + i) % ny
        return pltpu.make_async_remote_copy(
            src_ref=dst.at[frm],
            dst_ref=dst.at[frm],
            send_sem=rsem.at[frm],
            recv_sem=rsem.at[frm],
            device_id={"seq_0": frm},
            device_id_type=MESH,
        )

    def row_arrival(dst, rsem, i):
        frm = (r + i) % nr
        return pltpu.make_async_remote_copy(
            src_ref=dst.at[frm],
            dst_ref=dst.at[frm],
            send_sem=rsem.at[frm],
            recv_sem=rsem.at[frm],
            device_id=row_peer(frm),
            device_id_type=MESH,
        )

    sends = []

    def go(copy):
        copy.start()
        sends.append(copy)

    def flipped(ref):
        return ref[...].T

    def head(h):
        return slice(h * width, (h + 1) * width)

    loads[1].wait()
    k_t = flipped(k_v)
    loads[2].wait()
    loads[3].wait()
    q_t = flipped(q_v)
    loads[4].wait()
    for h in range(nh):
        kw = (k_t[head(h), :].astype(F32) * down_decay[h : h + 1, :]).astype(BF16)
        qw = (q_t[head(h), :].astype(F32) * up_decay[h : h + 1, :]).astype(BF16)
        buf_a[h, :, 0] = nn(kw, v_v[:, head(h)]).astype(BF16).reshape(nr, part, width)
        buf_a[h, :, 1] = nn(qw, g_v[:, head(h)]).astype(BF16).reshape(nr, part, width)

    pl.semaphore_wait(barrier, nr + ny)
    for i in far_first(nr):
        go(row_copy(lbuf_a, lrec_a.at[r], sla_sem.at[i - 1], rla_sem.at[r], i))
    lrec_a[r] = lbuf_a[...]
    for h in range(nh):
        for i in far_first(nr):
            go(row_copy(buf_a.at[h, (r + i) % nr], rec_a.at[h, r], sa_sem.at[h, i - 1], ra_sem.at[h, r], i))
        rec_a[h, r] = buf_a[h, r]

    for i in range(1, nr):
        row_arrival(lrec_a, rla_sem, i).wait_recv()
    ahead = jnp.zeros((8, LANES), F32)
    for p in range(nr):
        wgt[0, p] = jnp.exp(ahead)
        wgt[2, p] = jnp.exp(lrec_a[p])
        ahead = ahead + lrec_a[p]
    lbuf_b[...] = ahead
    for i in far_first(ny):
        go(column_copy(lbuf_b, lrec_b.at[y], slb_sem.at[i - 1], rlb_sem.at[y], i))
    behind = jnp.zeros((8, LANES), F32)
    for p in reversed(range(nr)):
        wgt[1, p] = jnp.exp(behind)
        behind = behind + lrec_a[p]

    cum_t = cum.T

    def local_part(h):
        gap = cum[h : h + 1, :] - cum_t[:, h : h + 1]
        decay = jnp.where(causal, jnp.exp(jnp.minimum(gap, 0.0)), 0.0)
        weighted = (nt(v_v[:, head(h)], g_v[:, head(h)]) * decay).astype(BF16)
        loc[0, h] = nn(k_t[head(h), :], weighted)
        loc[1, h] = nt(q_t[head(h), :], weighted)

    local_part(0)

    for h in range(nh):
        for i in range(1, nr):
            row_arrival(rec_a.at[h], ra_sem.at[h], i).wait_recv()
        run = jnp.zeros((part, width), F32)
        for p in range(nr):
            exc[h, 0, p] = run
            run = wgt[2, p, h : h + 1, :] * run + rec_a[h, p, 0].astype(F32)
        tot_b[h, 0] = run.astype(BF16)
        run = jnp.zeros((part, width), F32)
        for p in reversed(range(nr)):
            exc[h, 1, p] = run
            run = wgt[2, p, h : h + 1, :] * run + rec_a[h, p, 1].astype(F32)
        tot_b[h, 1] = run.astype(BF16)
        for i in far_first(ny):
            go(column_copy(tot_b.at[h, (y + i) // ny], rec_b.at[h, y], sb_sem.at[h, i - 1], rb_sem.at[h, y], i))
        rec_b[h, y] = jnp.zeros((part, width), BF16)

    for load in loads[5:]:
        load.start()

    for h in range(1, nh):
        local_part(h)
    g_t = flipped(g_v)
    v_t = flipped(v_v)

    lrec_b[y] = jnp.zeros((8, LANES), F32)
    for i in range(1, ny):
        column_arrival(lrec_b, rlb_sem, i).wait_recv()
    ahead = jnp.zeros((8, LANES), F32)
    for p in reversed(range(ny)):
        wgt_b[0, p] = jnp.where(p < y, jnp.exp(ahead), 0.0)
        ahead = ahead + jnp.where(p < y, lrec_b[p], 0.0)
    behind = jnp.zeros((8, LANES), F32)
    for p in range(ny):
        wgt_b[1, p] = jnp.where(p > y, jnp.exp(behind), 0.0)
        behind = behind + jnp.where(p > y, lrec_b[p], 0.0)

    for h in range(nh):
        for i in range(1, ny):
            column_arrival(rec_b.at[h], rb_sem.at[h], i).wait_recv()
        before = jnp.zeros((part, width), F32)
        after = jnp.zeros((part, width), F32)
        for p in range(ny):
            term = rec_b[h, p].astype(F32)
            before = before + wgt_b[0, p, h : h + 1, :] * term
            after = after + wgt_b[1, p, h : h + 1, :] * term
        for p in range(nr):
            buf_c[h, p, 0] = (wgt[0, p, h : h + 1, :] * before + exc[h, 0, p]).astype(BF16)
            buf_c[h, p, 1] = (wgt[1, p, h : h + 1, :] * after + exc[h, 1, p]).astype(BF16)
        for i in far_first(nr):
            go(row_copy(buf_c.at[h, (r + i) % nr], rec_c.at[h, r], sc_sem.at[h, i - 1], rc_sem.at[h, r], i))
        rec_c[h, r] = buf_c[h, r]

    def finish(h):
        for i in range(1, nr):
            row_arrival(rec_c.at[h], rc_sem.at[h], i).wait_recv()
        state = rec_c[h, :, 0].reshape(width, width)
        xt[head(h), :] = (loc[0, h] + nn(state, g_t[head(h), :]) * up_decay[h : h + 1, :]).astype(BF16)
        state = rec_c[h, :, 1].reshape(width, width)
        xt[head(nh + h), :] = (loc[1, h] + nn(state, v_t[head(h), :]) * down_decay[h : h + 1, :]).astype(BF16)

    mid = PIECES // 2
    most = (nh - 1) * width
    far = (z + half) % nz

    def some(pc, lo, hi):
        span_rows = pl.ds(pl.multiple_of(far * chunk + pc * rows, rows), rows)
        return nn(wq_v[span_rows, lo:hi], xt[lo:hi, :]) + nn(wk_v[span_rows, lo:hi], xt[hw + lo : hw + hi, :])

    for h in range(nh - 1):
        finish(h)
    loads[5].wait()
    loads[6].wait()
    for pc in range(PIECES):
        out_ref[pl.ds(pc * rows, rows), :] = some(pc, 0, most)
    finish(nh - 1)

    def own(dest, pc):
        span_rows = pl.ds(pl.multiple_of(dest * chunk + pc * rows, rows), rows)
        return nn(wq_v[span_rows, :], xt[0:hw, :]) + nn(wk_v[span_rows, :], xt[hw : 2 * hw, :])

    def ring_copy(way, step, pc):
        at = pl.ds(pc * rows, rows)
        return pltpu.make_async_remote_copy(
            src_ref=sbuf.at[way, step, at],
            dst_ref=rbuf.at[way, step, at],
            send_sem=sz_sem.at[way, step, pc],
            recv_sem=rz_sem.at[way, step, pc],
            device_id={"head": (z + (1 if way == 0 else nz - 1)) % nz},
            device_id_type=MESH,
        )

    def relay(way, step, pc, fresh):
        away = half - step
        dest = (z + (away if way == 0 else nz - away)) % nz
        value = own(dest, pc)
        at = pl.ds(pc * rows, rows)
        if not fresh:
            ring_copy(way, step - 1, pc).wait_recv()
            value = value + rbuf[way, step - 1, at, :].astype(F32)
        sbuf[way, step, at, :] = value.astype(BF16)
        ring_copy(way, step, pc).start()

    for i in range(mid):
        for way in range(2):
            pc = mid * way + i
            at = pl.ds(pc * rows, rows)
            sbuf[way, 0, at, :] = (out_ref[at, :] + some(pc, most, hw)).astype(BF16)
            ring_copy(way, 0, pc).start()
    for i in range(mid):
        relay(0, 1, mid + i, True)
        relay(1, 1, i, True)
    for i in range(mid):
        relay(0, 1, i, False)
        relay(1, 1, mid + i, False)

    def ring_step(step, carry):
        for i in range(PIECES):
            relay(0, step, (mid + i) % PIECES, False)
            relay(1, step, i, False)
        return carry

    lax.fori_loop(2, half, ring_step, 0)
    for pc in range(PIECES):
        out_ref[pl.ds(pc * rows, rows), :] = own(z, pc)
    for copy in sends:
        copy.wait_send()
    for way in range(2):
        for i in range(mid):
            ring_copy(way, 0, i + mid * way).wait_send()

    def drain(step, carry):
        for way in range(2):
            for pc in range(PIECES):
                ring_copy(way, step, pc).wait_send()
        return carry

    lax.fori_loop(1, half - 1, drain, 0)
    for i in range(PIECES):
        pc = i // 2 + mid * (i % 2)
        at = pl.ds(pc * rows, rows)
        for way in (i % 2, 1 - i % 2):
            ring_copy(1 - way, half - 1, pc).wait_recv()
            out_ref[at, :] += rbuf[1 - way, half - 1, at, :].astype(F32)

    for way in range(2):
        for pc in range(PIECES):
            ring_copy(way, half - 1, pc).wait_send()


def shards(sizes, query_act, key_act, value_act, grad_output, log_decay, w_query, w_key):
    ny, nx, nc, nz = sizes
    span = query_act.shape[0]
    nh = log_decay.shape[1]
    width = query_act.shape[1] // nh
    hw = nh * width
    nr = nx * nc
    part = width // nr
    half = nz // 2
    features = w_query.shape[0]
    chunk = features // nz
    dims = (ny, nr, nc, nz, nh, span, chunk)
    vmem = pltpu.VMEM
    dma = pltpu.SemaphoreType.DMA
    scratch = [
        vmem((span, hw), BF16), vmem((span, hw), BF16), vmem((span, hw), BF16), vmem((span, hw), BF16),
        vmem((nh, span), F32), vmem((features, hw), BF16), vmem((features, hw), BF16),
        vmem((nh, nr, 2, part, width), BF16), vmem((nh, nr, 2, part, width), BF16),
        vmem((8, LANES), F32), vmem((nr, 8, LANES), F32),
        vmem((nh, 2, nr, part, width), F32), vmem((3, nr, 8, LANES), F32), vmem((2, ny, 8, LANES), F32),
        vmem((nh, 2, part, width), BF16), vmem((nh, ny, part, width), BF16),
        vmem((8, LANES), F32), vmem((ny, 8, LANES), F32),
        vmem((nh, nr, 2, part, width), BF16), vmem((nh, nr, 2, part, width), BF16),
        vmem((2, nh, width, span), F32), vmem((2 * hw, span), BF16),
        vmem((2, half, chunk, span), BF16), vmem((2, half, chunk, span), BF16),
        dma((7,)),
        dma((nh, nr - 1)), dma((nh, nr)), dma((nr - 1,)), dma((nr,)),
        dma((nh, ny - 1)), dma((nh, ny)), dma((ny - 1,)), dma((ny,)),
        dma((nh, nr - 1)), dma((nh, nr)),
        dma((2, half, PIECES)), dma((2, half, PIECES)),
    ]
    hbm = pl.BlockSpec(memory_space=pl.ANY)
    total = pl.pallas_call(
        functools.partial(kernel, dims),
        out_shape=pltpu.VMEM((chunk, span), F32),
        in_specs=[hbm] * 7,
        out_specs=pl.BlockSpec(memory_space=pltpu.VMEM),
        scratch_shapes=scratch,
        compiler_params=pltpu.CompilerParams(
            collective_id=0, has_side_effects=True, vmem_limit_bytes=56 * 1024 * 1024
        ),
        name="attention_backward",
    )(query_act, key_act, value_act, grad_output, log_decay.T, w_query, w_key)
    return total.astype(BF16)


def build(torus):
    sizes = tuple(torus.shape[a] for a in SEQ + ("head",))
    return jax.shard_map(
        functools.partial(shards, sizes),
        mesh=torus,
        in_specs=(
            P(SEQ, "head"),
            P(SEQ, "head"),
            P(SEQ, "head"),
            P(SEQ, "head"),
            P(SEQ, "head"),
            P(None, "head"),
            P(None, "head"),
        ),
        out_specs=P("head", SEQ),
        check_vma=False,
    )


def solution(mesh):
    torus = Mesh(
        mesh.devices.reshape(8, 4, 2, mesh.shape["head"]), ("seq_0", "seq_1", "seq_2", "head")
    )
    return build(torus)
```
